512 devices in a mesh: box: 32 (over z, core), dir: 16 (over y, x).
Axes of the slice: x: 4, y: 4, z: 16, core: 2. Of those that a mesh axis runs over, the one named last changes fastest.
Arguments:
- fine_density: bfloat16 [4096, 6144], P(('box', 'dir')), may hold values from -6 to 6
- coarse_density: bfloat16 [2048, 12288], P(('box', 'dir')), may hold values from -6 to 6
- fine_operators: bfloat16 [192, 3072], replicated, may hold values from -0.109375 to 0.109375
- coarse_operators: bfloat16 [192, 3072], replicated, may hold values from -0.109375 to 0.109375
- fine_balance: int32 [32], replicated, may hold values from 0 to 31, each once
- coarse_balance: int32 [64], replicated, may hold values from 0 to 63, each once
- fine_sources: int32 [32, 65536], P('dir', 'box'), may hold values from 0 to 4095, as said below
- fine_targets: int32 [32, 65536], P('dir', 'box'), may hold values from 0 to 4095, as said below
- fine_op_ids: int32 [32, 65536], P('dir', 'box'), may hold values from 0 to 15
- coarse_sources: int32 [64, 32768], P('dir', 'box'), may hold values from 0 to 2047, as said below
- coarse_targets: int32 [64, 32768], P('dir', 'box'), may hold values from 0 to 2047, as said below
- coarse_op_ids: int32 [64, 32768], P('dir', 'box'), may hold values from 0 to 15
Outputs:
- fine_local: bfloat16 [4096, 6144], P('box', 'dir')
- coarse_local: bfloat16 [2048, 12288], P('box', 'dir')
The draws below stay inside these ranges and needn't reach their ends.
Inputs may be any that keep to these rules, and one draw needn't show every extreme that they name: `fine_targets`: pair column p belongs to the Morton range r = p // 2048; its target box lies in boxes r * 128 to (r + 1) * 128 - 1, and the first and last box of every range are named. `fine_sources`: the source of a pair of range r lies in boxes r * 128 - 32 to (r + 1) * 128 + 31, within the grid; in every range the sources at both ends of that span, as far as they lie in the grid, are named. `coarse_targets`: pair column p belongs to the Morton range r = p // 1024; its target box lies in boxes r * 64 to (r + 1) * 64 - 1, and the first and last box of every range are named. `coarse_sources`: the source of a pair of range r lies in boxes r * 64 - 32 to (r + 1) * 64 + 31, within the grid; in every range the sources at both ends of that span, as far as they lie in the grid, are named.
All inputs are finite; a program needn't handle non-finite values.
Results may differ from the reference program's by a relative error of at most 0.001.
Values may be sent and summed in bfloat16 or wider, within the bound.
No kernel may reach another device: no remote copies, remote signals or barrier semaphores. Data moves between devices by JAX's collectives and lax.ppermute only.
A program may use at most 64 MiB of HBM per device.

```python
import jax
import jax.numpy as jnp
from jax import lax

C = 192
NOP = 16
PPB = 16
RIM = 32
BPB1 = 128
BPB2 = 64
NB1 = 4096
NB2 = 2048
NW1 = 32
NW2 = 64
PAIRS1 = 65536
PAIRS2 = 32768


def target_draw(key, slots, pairs, per_range):
    column = jnp.arange(pairs, dtype=jnp.int32)
    lower = column // (PPB * per_range) * per_range
    within = column % (PPB * per_range)
    offsets = jax.random.randint(key, (slots, pairs), 0, per_range, dtype=jnp.int32)
    values = lower[None, :] + offsets
    values = jnp.where((within == 2)[None, :], (lower + per_range - 1)[None, :], values)
    values = jnp.where((within == 3)[None, :], lower[None, :], values)
    return values.astype(jnp.int32)


def source_draw(key, slots, pairs, per_range, total):
    column = jnp.arange(pairs, dtype=jnp.int32)
    lower = column // (PPB * per_range) * per_range
    within = column % (PPB * per_range)
    offsets = jax.random.randint(key, (slots, pairs), 0, per_range + 2 * RIM, dtype=jnp.int32)
    values = lower[None, :] - RIM + offsets
    values = jnp.where((within == 0)[None, :], (lower - RIM)[None, :], values)
    values = jnp.where((within == 1)[None, :], (lower + per_range + RIM - 1)[None, :], values)
    return jnp.clip(values, 0, total - 1).astype(jnp.int32)


def draw_fine_targets(key, part):
    return target_draw(jax.random.fold_in(key, 11), NW1, PAIRS1, BPB1)


def draw_fine_sources(key, part):
    return source_draw(jax.random.fold_in(key, 12), NW1, PAIRS1, BPB1, NB1)


def draw_coarse_targets(key, part):
    return target_draw(jax.random.fold_in(key, 13), NW2, PAIRS2, BPB2)


def draw_coarse_sources(key, part):
    return source_draw(jax.random.fold_in(key, 14), NW2, PAIRS2, BPB2, NB2)


def place_ends(drawn, stream_key, smallest, largest):
    extent = drawn.shape
    index_at = [jax.random.randint(jax.random.fold_in(stream_key, axis), (), 0, extent[axis]) for axis in range(len(extent))]
    drawn = drawn.at[tuple(index_at)].set(smallest)
    longest = extent.index(max(extent))
    index_at[longest] = (index_at[longest] + 1) % extent[longest]
    return drawn.at[tuple(index_at)].set(largest)


def level_of(stream_key, dims, shards, low, largest):
    def one(axis_at, parts):
        draws = jax.random.uniform(jax.random.fold_in(jax.random.fold_in(stream_key, 6), axis_at), (parts,), jnp.float32, low / len(shards), largest / len(shards))
        return jnp.repeat(jnp.exp(draws), dims[axis_at] // parts).reshape((-1,) + (1,) * (len(dims) - axis_at - 1))

    level = one(*shards[0])
    for cut in shards[1:]:
        level = level * one(*cut)
    return level


def noise(own_key, shape, deviation, bound, pieces=(), held_as=jnp.bfloat16):
    loudness = level_of(own_key, shape, pieces, -0.22, 0.18) if pieces else 1.0
    entries = jax.random.normal(own_key, shape, jnp.float32) * deviation * loudness
    return jnp.minimum(jnp.maximum(entries, -bound), bound).astype(held_as)


def setup_inputs(seed: int = 0) -> dict:
    key_of = jax.random.split(jax.random.key(seed), 13)
    return {
        "fine_density": noise(key_of[0], (NB1, NW1 * C), 1.0, 6.0, ((0, 512),)),
        "coarse_density": noise(key_of[1], (NB2, NW2 * C), 1.0, 6.0, ((0, 512),)),
        "fine_operators": noise(key_of[2], (C, NOP * C), (C * PPB) ** -0.5, 0.109375),
        "coarse_operators": noise(key_of[3], (C, NOP * C), (C * PPB) ** -0.5, 0.109375),
        "fine_balance": jax.random.permutation(key_of[4], NW1).astype(jnp.int32),
        "coarse_balance": jax.random.permutation(key_of[5], NW2).astype(jnp.int32),
        "fine_sources": draw_fine_sources(jax.random.fold_in(key_of[12], 71), 0),
        "fine_targets": draw_fine_targets(jax.random.fold_in(key_of[12], 71), 0),
        "fine_op_ids": place_ends(jax.random.randint(key_of[8], (NW1, PAIRS1), 0, NOP), jax.random.fold_in(key_of[8], 1), 0, NOP - 1).astype(jnp.int32),
        "coarse_sources": draw_coarse_sources(jax.random.fold_in(key_of[12], 71), 0),
        "coarse_targets": draw_coarse_targets(jax.random.fold_in(key_of[12], 71), 0),
        "coarse_op_ids": place_ends(jax.random.randint(key_of[11], (NW2, PAIRS2), 0, NOP), jax.random.fold_in(key_of[11], 1), 0, NOP - 1).astype(jnp.int32),
    }


def one_level(density, operators, balance, sources, targets, op_ids):
    channel = operators.shape[0]
    op_count = operators.shape[1] // channel
    box_count = density.shape[0]
    wedge_count = density.shape[1] // channel
    shaped = density.reshape(box_count, wedge_count, channel)
    sorted_slots = jnp.take(shaped, balance, axis=1)
    operators_wide = operators.astype(jnp.float32).reshape(channel, op_count, channel)

    def per_slot(packed):
        column, source_row, target_row, op_row = packed
        lookup = jnp.einsum("bc,cod->bod", column.astype(jnp.float32), operators_wide)
        picked = lookup.reshape(box_count * op_count, channel)[source_row * op_count + op_row]
        summed = jax.ops.segment_sum(picked, target_row, num_segments=box_count)
        return summed.astype(jnp.bfloat16)

    result = lax.map(per_slot, (jnp.transpose(sorted_slots, (1, 0, 2)), sources, targets, op_ids))
    return jnp.transpose(result, (1, 0, 2)).reshape(box_count, wedge_count * channel)


def reference(fine_density, coarse_density, fine_operators, coarse_operators, fine_balance, coarse_balance, fine_sources, fine_targets, fine_op_ids, coarse_sources, coarse_targets, coarse_op_ids):
    fine_local = one_level(fine_density, fine_operators, fine_balance, fine_sources, fine_targets, fine_op_ids)
    coarse_local = one_level(coarse_density, coarse_operators, coarse_balance, coarse_sources, coarse_targets, coarse_op_ids)
    return (fine_local, coarse_local)
```

```python
import functools

import jax
import jax.numpy as jnp
from jax import lax
from jax.experimental import pallas as pl
from jax.experimental.pallas import tpu as pltpu
from jax.sharding import PartitionSpec as P

RIM = 32
C = 192
NOP = 16
BF = jnp.bfloat16
F32 = jnp.float32


def pack_kernel(fine_balance, coarse_balance, fine_ref, coarse_ref, out_ref, fine_wide, coarse_wide):
    peers = out_ref.shape[0]
    fine_wide[...] = fine_ref[...].astype(F32)
    coarse_half = coarse_ref[...].astype(F32)
    coarse_wide[0:4, :] = coarse_half
    coarse_wide[4:8, :] = coarse_half
    low = lax.broadcasted_iota(jnp.int32, (8, 128), 1) < 64
    top = lax.broadcasted_iota(jnp.int32, (8, 128), 0) < 4

    def window(ref, wedge):
        odd = lax.rem(wedge, 2)
        start = pl.multiple_of(wedge * C - odd * 64, 128)
        first = ref[:, pl.ds(start, 128)]
        second = ref[:, pl.ds(pl.multiple_of(start + 128, 128), 128)]
        return odd == 1, first, second, pltpu.roll(first, 64, 1), pltpu.roll(second, 64, 1)

    def left(ref, wedge):
        odd, first, second, first_r, second_r = window(ref, wedge)
        head = jnp.where(odd, jnp.where(low, first_r, second_r), first)
        return head, jnp.where(odd, second_r, second)

    def right(ref, wedge):
        odd, first, second, first_r, second_r = window(ref, wedge)
        tail = jnp.where(odd, second, jnp.where(low, first_r, second_r))
        return jnp.where(odd, first, first_r), tail

    def joined(even, odd):
        return even[0], jnp.where(low, even[1], odd[0]), odd[1]

    for peer in range(peers):
        parts = joined(left(fine_wide, fine_balance[2 * peer]), right(fine_wide, fine_balance[2 * peer + 1]))
        upper = joined(left(coarse_wide, coarse_balance[4 * peer]), right(coarse_wide, coarse_balance[4 * peer + 1]))
        lower = joined(left(coarse_wide, coarse_balance[4 * peer + 2]), right(coarse_wide, coarse_balance[4 * peer + 3]))
        for k in range(3):
            out_ref[peer, 0:8, k * 128 : (k + 1) * 128] = parts[k].astype(BF)
            out_ref[peer, 8:16, k * 128 : (k + 1) * 128] = jnp.where(top, upper[k], lower[k]).astype(BF)


def pack(fine_balance, coarse_balance, fine_density, coarse_density, peers):
    whole = lambda a: pl.BlockSpec(a.shape, lambda i, *_: (0,) * a.ndim)
    return pl.pallas_call(
        pack_kernel,
        out_shape=jax.ShapeDtypeStruct((peers, 16, 2 * C), BF),
        grid_spec=pltpu.PrefetchScalarGridSpec(
            num_scalar_prefetch=2,
            grid=(1,),
            in_specs=[whole(fine_density), whole(coarse_density)],
            out_specs=pl.BlockSpec((peers, 16, 2 * C), lambda i, *_: (0, 0, 0)),
            scratch_shapes=[
                pltpu.VMEM((8, fine_density.shape[1]), F32),
                pltpu.VMEM((8, coarse_density.shape[1]), F32),
            ],
        ),
        compiler_params=pltpu.CompilerParams(vmem_limit_bytes=8 << 20),
        name="pack",
    )(fine_balance, coarse_balance, fine_density, coarse_density)


def count_level(slot, first, src_ref, tgt_ref, op_ref, out_ref, high_ref, flag_ref, tt, st, boxes, group):
    pairs = src_ref.shape[1]
    span = boxes + 2 * RIM
    target = tgt_ref[pl.ds(slot, 1), :] - first
    source = src_ref[pl.ds(slot, 1), :] - (first - RIM)
    tt[...] = (lax.broadcasted_iota(jnp.int32, (boxes, pairs), 0) == target).astype(F32).astype(BF)
    hot = (lax.broadcasted_iota(jnp.int32, (span, pairs), 0) == source).astype(F32)
    st[...] = hot.T.astype(BF)
    op_rows = jnp.broadcast_to(op_ref[pl.ds(slot, 1), :], (16, pairs))

    def one_group(g, most):
        parts = []
        for k in range(group):
            mask = (op_rows == g * group + k).astype(F32).astype(BF)
            parts.append((tt[...].reshape(boxes // 16, 16, pairs) * mask[None]).reshape(boxes, pairs))
        lhs = jnp.concatenate(parts, axis=0)
        count = jnp.dot(lhs, st[...], preferred_element_type=F32)
        high = jnp.floor(count * (1.0 / 256.0))
        rows = pl.ds(pl.multiple_of(g * group * boxes, 128), group * boxes)
        out_ref[slot, rows, :] = (count - high * 256.0).astype(BF)
        high_ref[slot, rows, :] = high.astype(BF)
        return jnp.maximum(most, jnp.max(count))

    most = lax.fori_loop(0, NOP // group, one_group, jnp.float32(0.0))
    flag_ref[0] = jnp.maximum(flag_ref[0], (most >= 256.0).astype(jnp.int32))


def count_kernel(
    firsts, fs, ft, fo, cs, ct, co, fop, cop, fn, fh, cn, ch, flag_ref, fops, cops, ftt, fst, ctt, cst
):
    flag_ref[0] = 0
    flag_ref[1] = 0
    for op_ref, ops_ref in ((fop, fops), (cop, cops)):
        for o in range(NOP):
            ops_ref[o] = op_ref[:, o * C : (o + 1) * C]
    lax.fori_loop(
        0,
        fs.shape[0],
        lambda j, _: (count_level(j, firsts[0], fs, ft, fo, fn, fh, flag_ref.at[pl.ds(0, 1)], ftt, fst, 128, 4), 0)[1],
        0,
    )
    lax.fori_loop(
        0,
        cs.shape[0],
        lambda j, _: (count_level(j, firsts[1], cs, ct, co, cn, ch, flag_ref.at[pl.ds(1, 1)], ctt, cst, 64, 8), 0)[1],
        0,
    )


def counts(firsts, fine_index, coarse_index, fine_operators, coarse_operators, fine_boxes, coarse_boxes):
    fine_slots, fine_pairs = fine_index[0].shape
    coarse_slots, coarse_pairs = coarse_index[0].shape
    fine_shape = (fine_slots, NOP * fine_boxes, fine_boxes + 2 * RIM)
    coarse_shape = (coarse_slots, NOP * coarse_boxes, coarse_boxes + 2 * RIM)
    vmem = pl.BlockSpec(memory_space=pltpu.VMEM)
    smem = pl.BlockSpec(memory_space=pltpu.SMEM)
    sds = jax.ShapeDtypeStruct
    return pl.pallas_call(
        count_kernel,
        out_shape=(
            sds(fine_shape, BF),
            sds(fine_shape, BF),
            sds(coarse_shape, BF),
            sds(coarse_shape, BF),
            sds((2,), jnp.int32),
            sds((NOP, C, C), BF),
            sds((NOP, C, C), BF),
        ),
        in_specs=[smem] + [vmem] * 8,
        out_specs=(vmem, vmem, vmem, vmem, smem, vmem, vmem),
        scratch_shapes=[
            pltpu.VMEM((fine_boxes, fine_pairs), BF),
            pltpu.VMEM((fine_pairs, fine_shape[2]), BF),
            pltpu.VMEM((coarse_boxes, coarse_pairs), BF),
            pltpu.VMEM((coarse_pairs, coarse_shape[2]), BF),
        ],
        compiler_params=pltpu.CompilerParams(vmem_limit_bytes=40 << 20),
        cost_estimate=pl.CostEstimate(flops=6_000_000_000, bytes_accessed=8_000_000, transcendentals=0),
        name="counts",
    )(firsts, *fine_index, *coarse_index, fine_operators, coarse_operators)


def apply_level(columns, n_ref, h_ref, flag, ops_ref, out_ref, high_part, low_part, boxes):
    slots = len(columns)
    rows = NOP * boxes
    chunk = 512
    per = chunk // boxes

    def place(value, c, slot):
        high = value.astype(BF)
        low = (value - high.astype(F32)).astype(BF)
        for k in range(per):
            high_part[c * per + k, slot * boxes : (slot + 1) * boxes, :] = high[k * boxes : (k + 1) * boxes]
            low_part[c * per + k, slot * boxes : (slot + 1) * boxes, :] = low[k * boxes : (k + 1) * boxes]

    for slot in range(slots):
        x = columns[slot]

        def plain(c, _, slot=slot, x=x):
            at = pl.ds(pl.multiple_of(c * chunk, chunk), chunk)
            place(jnp.dot(n_ref[slot, at, :], x, preferred_element_type=F32), c, slot)
            return 0

        def wide(c, _, slot=slot, x=x):
            at = pl.ds(pl.multiple_of(c * chunk, chunk), chunk)
            value = jnp.dot(n_ref[slot, at, :], x, preferred_element_type=F32)
            more = jnp.dot(h_ref[slot, at, :], x, preferred_element_type=F32)
            place(value + 256.0 * more, c, slot)
            return 0

        @pl.when(flag == 0)
        def _(plain=plain):
            lax.fori_loop(0, rows // chunk, plain, 0)

        @pl.when(flag != 0)
        def _(wide=wide):
            lax.fori_loop(0, rows // chunk, wide, 0)

    def one_op(o, total):
        total = total + jnp.dot(high_part[o], ops_ref[o], preferred_element_type=F32)
        return total + jnp.dot(low_part[o], ops_ref[o], preferred_element_type=F32)

    total = lax.fori_loop(0, NOP, one_op, jnp.zeros((slots * boxes, C), F32))
    for pair in range(slots // 2):
        both = jnp.concatenate(
            [total[(2 * pair + k) * boxes : (2 * pair + k + 1) * boxes] for k in range(2)], axis=1
        )
        out_ref[:, pair * 2 * C : (pair + 1) * 2 * C] = both.astype(BF)


def apply_kernel(
    flag_ref, own, before, after, fn, fh, cn, ch, fops, cops, fine_out, coarse_out, fhi, flo, chi, clo
):
    def fine_rows(ref, lo, hi):
        return ref[lo:hi, 0:8, :].reshape((hi - lo) * 8, 2 * C)

    fine = jnp.concatenate([fine_rows(before, 4, 8), fine_rows(own, 0, 16), fine_rows(after, 0, 4)], axis=0)
    apply_level([fine[:, :C], fine[:, C:]], fn, fh, flag_ref[0], fops, fine_out, fhi, flo, 128)

    def coarse_rows(ref):
        value = ref[:, 8:16, :].astype(F32)
        value = value.reshape(value.shape[0] // 2, 2, 8, 2 * C)
        first, second = value[:, 0], value[:, 1]
        top = lax.broadcasted_iota(jnp.int32, first.shape, 1) < 4
        count = first.shape[0] * 8
        upper = jnp.where(top, first, pltpu.roll(second, 4, 1)).reshape(count, 2 * C)
        lower = jnp.where(top, pltpu.roll(first, 4, 1), second).reshape(count, 2 * C)
        return upper.astype(BF), lower.astype(BF)

    pieces = [coarse_rows(before), coarse_rows(own), coarse_rows(after)]
    columns = []
    for half in range(2):
        block = jnp.concatenate([p[half] for p in pieces], axis=0)
        columns += [block[:, :C], block[:, C:]]
    apply_level(columns, cn, ch, flag_ref[1], cops, coarse_out, chi, clo, 64)


def apply(flag, own, before, after, fn, fh, cn, ch, fops, cops, fine_boxes, coarse_boxes):
    vmem = pl.BlockSpec(memory_space=pltpu.VMEM)
    smem = pl.BlockSpec(memory_space=pltpu.SMEM)
    rows = fn.shape[0] * fine_boxes
    coarse_rows = cn.shape[0] * coarse_boxes
    return pl.pallas_call(
        apply_kernel,
        out_shape=(
            jax.ShapeDtypeStruct((fine_boxes, fn.shape[0] * C), BF),
            jax.ShapeDtypeStruct((coarse_boxes, cn.shape[0] * C), BF),
        ),
        in_specs=[smem] + [vmem] * 9,
        out_specs=(vmem, vmem),
        scratch_shapes=[
            pltpu.VMEM((NOP, rows, C), BF),
            pltpu.VMEM((NOP, rows, C), BF),
            pltpu.VMEM((NOP, coarse_rows, C), BF),
            pltpu.VMEM((NOP, coarse_rows, C), BF),
        ],
        compiler_params=pltpu.CompilerParams(vmem_limit_bytes=40 << 20),
        cost_estimate=pl.CostEstimate(flops=2_000_000_000, bytes_accessed=8_000_000, transcendentals=0),
        name="apply",
    )(flag, own, before, after, fn, fh, cn, ch, fops, cops)


def per_device(
    fine_density,
    coarse_density,
    fine_operators,
    coarse_operators,
    fine_balance,
    coarse_balance,
    fine_sources,
    fine_targets,
    fine_op_ids,
    coarse_sources,
    coarse_targets,
    coarse_op_ids,
):
    peers = lax.axis_size("dir")
    count = lax.axis_size("box")
    fine_boxes = fine_density.shape[0] * peers
    coarse_boxes = coarse_density.shape[0] * peers
    position = lax.axis_index("box")
    firsts = jnp.stack([position * fine_boxes, position * coarse_boxes]).astype(jnp.int32)
    packed = pack(fine_balance, coarse_balance, fine_density, coarse_density, peers)
    own = lax.all_to_all(packed, "dir", split_axis=0, concat_axis=0, tiled=True)
    fn, fh, cn, ch, flag, fops, cops = counts(
        firsts,
        (fine_sources, fine_targets, fine_op_ids),
        (coarse_sources, coarse_targets, coarse_op_ids),
        fine_operators,
        coarse_operators,
        fine_boxes,
        coarse_boxes,
    )
    up = [(i, i + 1) for i in range(count - 1)]
    down = [(i + 1, i) for i in range(count - 1)]
    half = peers // 2
    before = lax.ppermute(own[half:], "box", up)
    after = lax.ppermute(own[:half], "box", down)
    return apply(flag, own, before, after, fn, fh, cn, ch, fops, cops, fine_boxes, coarse_boxes)


def solution(mesh):
    placed = (
        P(("box", "dir"), None),
        P(("box", "dir"), None),
        P(),
        P(),
        P(),
        P(),
        P("dir", "box"),
        P("dir", "box"),
        P("dir", "box"),
        P("dir", "box"),
        P("dir", "box"),
        P("dir", "box"),
    )
    return jax.shard_map(
        per_device,
        mesh=mesh,
        in_specs=placed,
        out_specs=(P("box", "dir"), P("box", "dir")),
        check_vma=False,
    )
```

```python
import functools

import jax
import jax.numpy as jnp
from jax import lax
from jax.experimental import pallas as pl
from jax.experimental.pallas import tpu as pltpu
from jax.sharding import PartitionSpec as P

RIM = 32
C = 192
NOP = 16
BF = jnp.bfloat16
F32 = jnp.float32


F8 = jnp.float8_e4m3fn
HOT = F8
VMEM = pl.BlockSpec(memory_space=pltpu.VMEM)
SMEM = pl.BlockSpec(memory_space=pltpu.SMEM)
HBM = pl.BlockSpec(memory_space=pltpu.HBM)
ANY = pl.BlockSpec(memory_space=pl.ANY)


def fetch(pairs, sems, first=0):
    copies = [pltpu.make_async_copy(s, d, sems.at[first + i]) for i, (s, d) in enumerate(pairs)]
    for copy in copies:
        copy.start()
    return copies


def pack_kernel(fb, cb, fd, cd, fh, ch, out_ref, fb_s, cb_s, fd_v, cd_v, fh_v, ch_v, fine_wide, coarse_wide, sems):
    copies = fetch(((fb, fb_s), (cb, cb_s), (fd, fd_v), (cd, cd_v), (fh, fh_v), (ch, ch_v)), sems)
    for copy in copies:
        copy.wait()
    fine_wide[0:8, :] = fd_v[...].astype(F32)
    fine_wide[8:16, :] = fh_v[...].astype(F32)
    for k, ref in enumerate((cd_v, ch_v)):
        rows = ref[...].astype(F32)
        coarse_wide[8 * k : 8 * k + 4, :] = rows
        coarse_wide[8 * k + 4 : 8 * k + 8, :] = rows
    low = lax.broadcasted_iota(jnp.int32, (16, 128), 1) < 64
    top = (lax.broadcasted_iota(jnp.int32, (16, 128), 0) & 7) < 4

    def window(ref, wedge):
        odd = lax.rem(wedge, 2)
        start = pl.multiple_of(wedge * C - odd * 64, 128)
        first = ref[:, pl.ds(start, 128)]
        second = ref[:, pl.ds(pl.multiple_of(start + 128, 128), 128)]
        return odd == 1, first, second, pltpu.roll(first, 64, 1), pltpu.roll(second, 64, 1)

    def left(ref, wedge):
        odd, first, second, first_r, second_r = window(ref, wedge)
        head = jnp.where(odd, jnp.where(low, first_r, second_r), first)
        return head, jnp.where(odd, second_r, second)

    def right(ref, wedge):
        odd, first, second, first_r, second_r = window(ref, wedge)
        tail = jnp.where(odd, second, jnp.where(low, first_r, second_r))
        return jnp.where(odd, first, first_r), tail

    def joined(even, odd):
        return even[0], jnp.where(low, even[1], odd[0]), odd[1]

    for peer in range(out_ref.shape[0]):
        parts = joined(left(fine_wide, fb_s[2 * peer]), right(fine_wide, fb_s[2 * peer + 1]))
        upper = joined(left(coarse_wide, cb_s[4 * peer]), right(coarse_wide, cb_s[4 * peer + 1]))
        lower = joined(left(coarse_wide, cb_s[4 * peer + 2]), right(coarse_wide, cb_s[4 * peer + 3]))
        for k in range(3):
            lanes = slice(k * 128, (k + 1) * 128)
            out_ref[peer, 0:16, lanes] = parts[k].astype(BF)
            out_ref[peer, 16:32, lanes] = jnp.where(top, upper[k], lower[k]).astype(BF)


def pack(fine_balance, coarse_balance, fine, coarse, fine_near, coarse_near, peers):
    arrays = (fine, coarse, fine_near, coarse_near)
    return pl.pallas_call(
        pack_kernel,
        out_shape=jax.ShapeDtypeStruct((peers, 32, 2 * C), BF),
        in_specs=[HBM] * 4 + [ANY] * 2,
        out_specs=VMEM,
        scratch_shapes=[pltpu.SMEM(fine_balance.shape, jnp.int32), pltpu.SMEM(coarse_balance.shape, jnp.int32)]
        + [pltpu.VMEM(a.shape, BF) for a in arrays]
        + [
            pltpu.VMEM((16, fine.shape[1]), F32),
            pltpu.VMEM((16, coarse.shape[1]), F32),
            pltpu.SemaphoreType.DMA((6,)),
        ],
        cost_estimate=pl.CostEstimate(flops=4_000_000, bytes_accessed=800_000, transcendentals=0),
        name="pack",
    )(fine_balance, coarse_balance, *arrays)


def op_groups(boxes):
    many = 512 // boxes
    groups = []
    for start in range(0, NOP, 2 * many):
        groups.append([start + 2 * k for k in range(many)])
        groups.append([start + 2 * k + 1 for k in range(many)])
    return groups


def count_slot(slot, column, src_ref, tgt_ref, op_ref, first, n_ref, h_ref, outs, sem, flag_ref, flag_at, tt, st, boxes):
    pairs = src_ref.shape[1]
    target = tgt_ref[pl.ds(slot, 1), :] - first
    source = column(src_ref[pl.ds(slot, 1), :] - first)
    tt[...] = (lax.broadcasted_iota(jnp.int32, (boxes, pairs), 0) == target).astype(F32).astype(BF)
    st[...] = (lax.broadcasted_iota(jnp.int32, (256, pairs), 0) == source).astype(F32).astype(HOT)
    op_rows = jnp.broadcast_to(op_ref[pl.ds(slot, 1), :], (16, pairs))

    def count(ops):
        parts = []
        for o in ops:
            mask = (op_rows == o).astype(F32).astype(BF)
            parts.append((tt[...].reshape(boxes // 16, 16, pairs) * mask[None]).reshape(boxes, pairs).astype(HOT))
        lhs = jnp.concatenate(parts, axis=0)
        return lax.dot_general(lhs, st[...], (((1,), (1,)), ((), ())), preferred_element_type=F32)

    most = jnp.float32(0.0)
    for g, ops in enumerate(op_groups(boxes)):
        found = count(ops)
        n_ref[slot, g * 512 : (g + 1) * 512, :] = found.astype(BF)
        most = jnp.maximum(most, jnp.max(found))
    many = most > 256.0
    flag_ref[flag_at + slot] = many.astype(jnp.int32)

    @pl.when(many)
    def _():
        for g, ops in enumerate(op_groups(boxes)):
            found = count(ops)
            high = jnp.floor(found * (1.0 / 256.0))
            n_ref[slot, g * 512 : (g + 1) * 512, :] = (found - high * 256.0).astype(BF)
            h_ref[g * 512 : (g + 1) * 512, :] = high.astype(BF)
        pltpu.sync_copy(h_ref, outs[1].at[slot])

    pltpu.make_async_copy(n_ref.at[slot], outs[0].at[slot], sem).start()


def fine_column(at):
    halo = jnp.logical_or(at < 0, at >= 128).astype(jnp.int32)
    return ((at & 127) >> 3) * 16 + halo * 8 + (at & 7)


def coarse_column(half):
    def column(at):
        halo = jnp.logical_or(at < 0, at >= 64).astype(jnp.int32)
        return ((at & 63) >> 2) * 16 + halo * 8 + half * 4 + (at & 3)

    return column


def count_kernel(
    firsts, fs, ft, fo, cs, ct, co, fop, cop, fn, fh, cn, ch, flag_ref, fw, cw,
    fs_v, ft_v, fo_v, cs_v, ct_v, co_v, fop_v, cop_v, ftt, fst, ctt, cst,
    fn_v, fh_v, cn_v, ch_v, fw_v, cw_v, sems, out_sems,
):
    copies = fetch(
        ((fs, fs_v), (ft, ft_v), (fo, fo_v), (cs, cs_v), (ct, ct_v), (co, co_v), (fop, fop_v), (cop, cop_v)), sems
    )
    for copy in copies[:6]:
        copy.wait()
    fine_slots, coarse_slots = fs_v.shape[0], cs_v.shape[0]

    def fine(j, _):
        outs, sem = (fn, fh), out_sems.at[j]
        count_slot(j, fine_column, fs_v, ft_v, fo_v, firsts[0], fn_v, fh_v, outs, sem, flag_ref, 0, ftt, fst, 128)
        return 0

    def coarse(j, _):
        outs, sem = (cn, ch), out_sems.at[fine_slots + j]
        column = coarse_column(j >> 1)
        count_slot(
            j, column, cs_v, ct_v, co_v, firsts[1], cn_v, ch_v, outs, sem, flag_ref, fine_slots, ctt, cst, 64
        )
        return 0

    lax.fori_loop(0, fine_slots, fine, 0)
    lax.fori_loop(0, coarse_slots, coarse, 0)
    total = fine_slots + coarse_slots
    done = [pltpu.make_async_copy(fn_v.at[j], fn.at[j], out_sems.at[j]) for j in range(fine_slots)]
    done += [pltpu.make_async_copy(cn_v.at[j], cn.at[j], out_sems.at[fine_slots + j]) for j in range(coarse_slots)]
    for k, (op_ref, w_v, w_ref) in enumerate(((fop_v, fw_v, fw), (cop_v, cw_v, cw))):
        copies[6 + k].wait()
        for o in range(NOP):
            w_v[o * C : (o + 1) * C, :] = op_ref[:, o * C : (o + 1) * C]
        done += fetch(((w_v, w_ref),), out_sems, total + k)
    for copy in done:
        copy.wait()


def counts(firsts, fine_index, coarse_index, fine_operators, coarse_operators, fine_boxes, coarse_boxes):
    fine_slots, fine_pairs = fine_index[0].shape
    coarse_slots, coarse_pairs = coarse_index[0].shape
    fine_shape = (fine_slots, NOP * fine_boxes, 256)
    coarse_shape = (coarse_slots, NOP * coarse_boxes, 256)
    sds = jax.ShapeDtypeStruct
    arrays = (*fine_index, *coarse_index, fine_operators, coarse_operators)
    return pl.pallas_call(
        count_kernel,
        out_shape=(
            sds(fine_shape, BF),
            sds(fine_shape, BF),
            sds(coarse_shape, BF),
            sds(coarse_shape, BF),
            sds((fine_slots + coarse_slots,), jnp.int32),
            sds((NOP * C, C), BF),
            sds((NOP * C, C), BF),
        ),
        in_specs=[SMEM] + [HBM] * 8,
        out_specs=(HBM, HBM, HBM, HBM, SMEM, HBM, HBM),
        scratch_shapes=[pltpu.VMEM(a.shape, a.dtype) for a in arrays]
        + [
            pltpu.VMEM((fine_boxes, fine_pairs), BF),
            pltpu.VMEM((256, fine_pairs), HOT),
            pltpu.VMEM((coarse_boxes, coarse_pairs), BF),
            pltpu.VMEM((256, coarse_pairs), HOT),
            pltpu.VMEM(fine_shape, BF),
            pltpu.VMEM(fine_shape[1:], BF),
            pltpu.VMEM(coarse_shape, BF),
            pltpu.VMEM(coarse_shape[1:], BF),
            pltpu.VMEM((NOP * C, C), BF),
            pltpu.VMEM((NOP * C, C), BF),
            pltpu.SemaphoreType.DMA((8,)),
            pltpu.SemaphoreType.DMA((fine_slots + coarse_slots + 2,)),
        ],
        cost_estimate=pl.CostEstimate(flops=9_000_000_000, bytes_accessed=8_000_000, transcendentals=0),
        name="counts",
    )(firsts, *arrays)


def place(value, high_part, low_part, rows, lanes):
    high = value.astype(BF)
    high_part[rows, lanes] = high
    low_part[rows, lanes] = (value - high.astype(F32)).astype(BF)


def apply_level(recv, base, slots, n_ref, h_hbm, waits, flag_ref, flag_at, w_ref, w_wait, out_ref, parts, boxes):
    high_part, low_part, total_ref, sem = parts
    lane = lax.broadcasted_iota(jnp.int32, (256, 256), 1)
    many = 512 // boxes
    steps = NOP // (2 * many)

    def sources(slot):
        at = (slot % 2) * 128
        block = recv[:, base : base + 16, at : at + 256].reshape(256, 256).astype(F32)
        turned = pltpu.roll(block, 64 if slot % 2 == 0 else 192, 1)
        left, right = (block, turned) if slot % 2 == 0 else (turned, block)
        return jnp.where(lane < C, left, 0.0).astype(BF), jnp.where(lane >= 64, right, 0.0).astype(BF)

    def split(slot, sides, g):
        start = g * 1024
        at = [pl.ds(start + k * 512 if isinstance(g, int) else pl.multiple_of(start + k * 512, 512), 512) for k in range(2)]
        even = jnp.dot(n_ref[slot, at[0], :], sides[0], preferred_element_type=F32)
        odd = jnp.dot(n_ref[slot, at[1], :], sides[1], preferred_element_type=F32)
        value = jnp.concatenate([even[:, :128], even[:, 128:] + odd[:, :128], odd[:, 128:]], axis=1)
        for k in range(many):
            lanes = (g * many + k) * 2 * C
            lanes = pl.ds(lanes if isinstance(g, int) else pl.multiple_of(lanes, 128), 2 * C)
            rows = slice(slot * boxes, (slot + 1) * boxes)
            place(value[k * boxes : (k + 1) * boxes], high_part, low_part, rows, lanes)

    for slot in range(slots):
        sides = sources(slot)
        for g in range(steps):
            waits[slot][g].wait()
            split(slot, sides, g)
    w_wait.wait()
    w = w_ref[...]
    total = jnp.dot(high_part[...], w, preferred_element_type=F32)
    total_ref[...] = total + jnp.dot(low_part[...], w, preferred_element_type=F32)
    some = flag_ref[flag_at]
    for slot in range(1, slots):
        some = some + flag_ref[flag_at + slot]

    @pl.when(some > 0)
    def _():
        for slot in range(slots):
            rows = slice(slot * boxes, (slot + 1) * boxes)
            high_part[rows, :] = jnp.zeros((boxes, NOP * C), BF)
            low_part[rows, :] = jnp.zeros((boxes, NOP * C), BF)

            @pl.when(flag_ref[flag_at + slot] > 0)
            def _(slot=slot):
                copy = pltpu.make_async_copy(h_hbm.at[slot], n_ref.at[slot], sem)
                copy.start()
                copy.wait()
                sides = sources(slot)
                lax.fori_loop(0, steps, lambda g, _: (split(slot, sides, g), 0)[1], 0)

        def more(k, _):
            at = pl.ds(pl.multiple_of(k * 256, 256), 256)
            extra = jnp.dot(high_part[:, at], w_ref[at, :], preferred_element_type=F32)
            extra = extra + jnp.dot(low_part[:, at], w_ref[at, :], preferred_element_type=F32)
            total_ref[...] = total_ref[...] + 256.0 * extra
            return 0

        lax.fori_loop(0, NOP * C // 256, more, 0)

    for pair in range(slots // 2):
        two = [total_ref[(2 * pair + k) * boxes : (2 * pair + k + 1) * boxes, :] for k in range(2)]
        out_ref[:, pair * 2 * C : (pair + 1) * 2 * C] = jnp.concatenate(two, axis=1).astype(BF)


def apply_kernel(
    flag_ref, recv, fn, fh, cn, ch, fw, cw, fine_out, coarse_out,
    recv_v, fn_v, cn_v, fw_v, cw_v, fine_v, coarse_v, high_part, low_part, total, sems,
):
    fine_slots, coarse_slots = fn.shape[0], cn.shape[0]
    at = 0

    def begin(source, target):
        nonlocal at
        copy = pltpu.make_async_copy(source, target, sems.at[at])
        copy.start()
        at += 1
        return copy

    def chunks(n_ref, n_v, slot):
        rows = [slice(g * 1024, (g + 1) * 1024) for g in range(n_ref.shape[1] // 1024)]
        return [begin(n_ref.at[slot, r, :], n_v.at[slot, r, :]) for r in rows]

    first = begin(recv, recv_v)
    fine_waits = [chunks(fn, fn_v, j) for j in range(fine_slots)]
    fine_w = begin(fw, fw_v)
    coarse_waits = [chunks(cn, cn_v, j) for j in range(coarse_slots)]
    coarse_w = begin(cw, cw_v)
    first.wait()
    parts = (high_part, low_part, total, sems.at[at])
    at += 1
    apply_level(recv_v, 0, fine_slots, fn_v, fh, fine_waits, flag_ref, 0, fw_v, fine_w, fine_v, parts, 128)
    out = begin(fine_v, fine_out)
    apply_level(
        recv_v, 16, coarse_slots, cn_v, ch, coarse_waits, flag_ref, fine_slots, cw_v, coarse_w, coarse_v, parts, 64
    )
    last = begin(coarse_v, coarse_out)
    out.wait()
    last.wait()


def apply(flag, recv, fn, fh, cn, ch, fw, cw, fine_boxes, coarse_boxes):
    rows = fn.shape[0] * fine_boxes
    outs = (
        jax.ShapeDtypeStruct((fine_boxes, fn.shape[0] * C), BF),
        jax.ShapeDtypeStruct((coarse_boxes, cn.shape[0] * C), BF),
    )
    return pl.pallas_call(
        apply_kernel,
        out_shape=outs,
        in_specs=[SMEM] + [HBM] * 7,
        out_specs=(HBM, HBM),
        scratch_shapes=[pltpu.VMEM(a.shape, BF) for a in (recv, fn, cn, fw, cw, *outs)]
        + [
            pltpu.VMEM((rows, NOP * C), BF),
            pltpu.VMEM((rows, NOP * C), BF),
            pltpu.VMEM((rows, C), F32),
            pltpu.SemaphoreType.DMA((24,)),
        ],
        cost_estimate=pl.CostEstimate(flops=3_000_000_000, bytes_accessed=8_000_000, transcendentals=0),
        name="apply",
    )(flag, recv, fn, fh, cn, ch, fw, cw)


def per_device(
    fine_density,
    coarse_density,
    fine_operators,
    coarse_operators,
    fine_balance,
    coarse_balance,
    fine_sources,
    fine_targets,
    fine_op_ids,
    coarse_sources,
    coarse_targets,
    coarse_op_ids,
):
    peers = lax.axis_size("dir")
    count = lax.axis_size("box")
    half = peers // 2
    fine_boxes = fine_density.shape[0] * peers
    coarse_boxes = coarse_density.shape[0] * peers
    position = lax.axis_index("box")
    firsts = jnp.stack([position * fine_boxes, position * coarse_boxes]).astype(jnp.int32)
    route = [(b * peers + d, (b + 1) * peers + d) for b in range(count - 1) for d in range(half, peers)]
    route += [(b * peers + d, (b - 1) * peers + d) for b in range(1, count) for d in range(half)]
    coarse_near = lax.ppermute(coarse_density, ("box", "dir"), route)
    fine_near = lax.ppermute(fine_density, ("box", "dir"), route)
    packed = pack(fine_balance, coarse_balance, fine_density, coarse_density, fine_near, coarse_near, peers)
    firsts, packed = lax.optimization_barrier((firsts, packed))
    recv = lax.all_to_all(packed, "dir", split_axis=0, concat_axis=0, tiled=True)
    fn, fh, cn, ch, flag, fw, cw = counts(
        firsts,
        (fine_sources, fine_targets, fine_op_ids),
        (coarse_sources, coarse_targets, coarse_op_ids),
        fine_operators,
        coarse_operators,
        fine_boxes,
        coarse_boxes,
    )
    return apply(flag, recv, fn, fh, cn, ch, fw, cw, fine_boxes, coarse_boxes)


def solution(mesh):
    placed = (
        P(("box", "dir"), None),
        P(("box", "dir"), None),
        P(),
        P(),
        P(),
        P(),
        P("dir", "box"),
        P("dir", "box"),
        P("dir", "box"),
        P("dir", "box"),
        P("dir", "box"),
        P("dir", "box"),
    )
    return jax.shard_map(
        per_device,
        mesh=mesh,
        in_specs=placed,
        out_specs=(P("box", "dir"), P("box", "dir")),
        check_vma=False,
    )
```

```python
import functools

import jax
import jax.numpy as jnp
from jax import lax
from jax.experimental import pallas as pl
from jax.experimental.pallas import tpu as pltpu
from jax.sharding import PartitionSpec as P

RIM = 32
C = 192
NOP = 16
BF = jnp.bfloat16
F32 = jnp.float32


LIMIT = 50 << 20
BASE = 4096.0
VMEM = pl.BlockSpec(memory_space=pltpu.VMEM)
SMEM = pl.BlockSpec(memory_space=pltpu.SMEM)
HBM = pl.BlockSpec(memory_space=pltpu.HBM)
ANY = pl.BlockSpec(memory_space=pl.ANY)


def fetch(pairs, sems, first=0):
    copies = [pltpu.make_async_copy(s, d, sems.at[first + i]) for i, (s, d) in enumerate(pairs)]
    for copy in copies:
        copy.start()
    return copies


def pack_kernel(fb, cb, fd, cd, fh, ch, out_ref, fb_s, cb_s, fd_v, cd_v, fh_v, ch_v, fine_wide, coarse_wide, sems):
    copies = fetch(((fb, fb_s), (cb, cb_s), (fd, fd_v), (cd, cd_v), (fh, fh_v), (ch, ch_v)), sems)
    for copy in copies:
        copy.wait()
    fine_wide[0:8, :] = fd_v[...].astype(F32)
    fine_wide[8:16, :] = fh_v[...].astype(F32)
    for k, ref in enumerate((cd_v, ch_v)):
        rows = ref[...].astype(F32)
        coarse_wide[8 * k : 8 * k + 4, :] = rows
        coarse_wide[8 * k + 4 : 8 * k + 8, :] = rows
    low = lax.broadcasted_iota(jnp.int32, (16, 128), 1) < 64
    top = (lax.broadcasted_iota(jnp.int32, (16, 128), 0) & 7) < 4

    def window(ref, wedge):
        odd = lax.rem(wedge, 2)
        start = pl.multiple_of(wedge * C - odd * 64, 128)
        first = ref[:, pl.ds(start, 128)]
        second = ref[:, pl.ds(pl.multiple_of(start + 128, 128), 128)]
        return odd == 1, first, second, pltpu.roll(first, 64, 1), pltpu.roll(second, 64, 1)

    def left(ref, wedge):
        odd, first, second, first_r, second_r = window(ref, wedge)
        head = jnp.where(odd, jnp.where(low, first_r, second_r), first)
        return head, jnp.where(odd, second_r, second)

    def right(ref, wedge):
        odd, first, second, first_r, second_r = window(ref, wedge)
        tail = jnp.where(odd, second, jnp.where(low, first_r, second_r))
        return jnp.where(odd, first, first_r), tail

    def joined(even, odd):
        return even[0], jnp.where(low, even[1], odd[0]), odd[1]

    for peer in range(out_ref.shape[0]):
        parts = joined(left(fine_wide, fb_s[2 * peer]), right(fine_wide, fb_s[2 * peer + 1]))
        upper = joined(left(coarse_wide, cb_s[4 * peer]), right(coarse_wide, cb_s[4 * peer + 1]))
        lower = joined(left(coarse_wide, cb_s[4 * peer + 2]), right(coarse_wide, cb_s[4 * peer + 3]))
        for k in range(3):
            lanes = slice(k * 128, (k + 1) * 128)
            out_ref[peer, 0:16, lanes] = parts[k].astype(BF)
            out_ref[peer, 16:32, lanes] = jnp.where(top, upper[k], lower[k]).astype(BF)


def pack(fine_balance, coarse_balance, fine, coarse, fine_near, coarse_near, peers):
    arrays = (fine, coarse, fine_near, coarse_near)
    return pl.pallas_call(
        pack_kernel,
        out_shape=jax.ShapeDtypeStruct((peers, 32, 2 * C), BF),
        in_specs=[HBM] * 4 + [ANY] * 2,
        out_specs=VMEM,
        scratch_shapes=[pltpu.SMEM(fine_balance.shape, jnp.int32), pltpu.SMEM(coarse_balance.shape, jnp.int32)]
        + [pltpu.VMEM(a.shape, BF) for a in arrays]
        + [
            pltpu.VMEM((16, fine.shape[1]), F32),
            pltpu.VMEM((16, coarse.shape[1]), F32),
            pltpu.SemaphoreType.DMA((6,)),
        ],
        cost_estimate=pl.CostEstimate(flops=4_000_000, bytes_accessed=800_000, transcendentals=0),
        name="pack",
    )(fine_balance, coarse_balance, *arrays)


def count_slot(slot, column, src_ref, tgt_ref, op_ref, first, n_ref, h_ref, table, plane, sem, flag_ref, flag_at, tt, st, boxes):
    pairs = src_ref.shape[1]
    rows = lambda v: jnp.broadcast_to(v, (16, pairs))
    steps = lax.broadcasted_iota(jnp.int32, (16, 128), 0).astype(F32)
    one, zero = jnp.ones((), BF), jnp.zeros((), BF)

    def hot(value, block):
        want = jnp.concatenate([(steps + 16.0 * block).astype(BF)] * (pairs // 128), axis=1)
        return jnp.where(value == want, one, zero)

    target = rows(tgt_ref[pl.ds(slot, 1), :] - first).astype(F32).astype(BF)
    source = rows(column(src_ref[pl.ds(slot, 1), :] - first)).astype(F32).astype(BF)
    for k in range(boxes // 16):
        tt[k * 16 : (k + 1) * 16, :] = hot(target, k)
    for k in range(st.shape[0] // 16):
        st[k * 16 : (k + 1) * 16, :] = hot(source, k)
    ops = rows(op_ref[pl.ds(slot, 1), :])
    member = ((ops & 1) * 4 + (ops >> 2)).astype(F32).astype(BF)
    factor = jnp.where((ops & 2) > 0, BASE, 1.0).astype(BF)
    many = 512 // boxes
    wide = st.shape[0] // 128
    planes = 8 // many * wide

    def store(ref, first, g, side, value):
        for k in range(wide):
            ref[first + g * wide + k, side * 512 : (side + 1) * 512, :] = value[:, k * 128 : (k + 1) * 128].astype(BF)

    def count(g):
        parts = []
        for k in range(many):
            mask = jnp.where(member == jnp.asarray(g * many + k, BF), factor, zero)
            part = tt[...].reshape(boxes // 16, 16, pairs) * mask[None]
            parts.append(part.reshape(boxes, pairs))
        lhs = jnp.concatenate(parts, axis=0)
        both = lax.dot_general(lhs, st[...], (((1,), (1,)), ((), ())), preferred_element_type=F32)
        second = jnp.floor(both * (1.0 / BASE))
        return both - second * BASE, second

    most = jnp.float32(0.0)
    for g in range(8 // many):
        found = count(g)
        for side in range(2):
            store(n_ref, plane, g, side, found[side])
        most = jnp.maximum(most, jnp.max(jnp.maximum(found[0], found[1])))
    big = most > 256.0
    flag_ref[pl.ds(flag_at + slot, 1), :] = jnp.full((1, 128), big.astype(F32))

    @pl.when(big)
    def _():
        for g in range(8 // many):
            found = count(g)
            for side in range(2):
                high = jnp.floor(found[side] * (1.0 / 256.0))
                store(n_ref, plane, g, side, found[side] - high * 256.0)
                store(h_ref, 0, g, side, high)
        pltpu.sync_copy(h_ref.at[pl.ds(0, planes)], table.at[pl.ds(n_ref.shape[0] + 1 + plane, planes)])

    pltpu.make_async_copy(n_ref.at[pl.ds(plane, planes)], table.at[pl.ds(plane, planes)], sem).start()


def fine_column(at):
    halo = jnp.logical_or(at < 0, at >= 128).astype(jnp.int32)
    return ((at & 127) >> 3) * 16 + halo * 8 + (at & 7)


def coarse_column(at):
    halo = jnp.logical_or(at < 0, at >= 64).astype(jnp.int32)
    return ((at & 63) >> 2) * 8 + halo * 4 + (at & 3)


def count_kernel(
    firsts, fs, ft, fo, cs, ct, co, table,
    fs_v, ft_v, fo_v, cs_v, ct_v, co_v, ftt, fst, ctt, cst, n_v, h_v, flag_ref, flag_v, sems, out_sems,
):
    copies = fetch(((fs, fs_v), (ft, ft_v), (fo, fo_v), (cs, cs_v), (ct, ct_v), (co, co_v)), sems)
    for copy in copies:
        copy.wait()
    fine_slots, coarse_slots = fs_v.shape[0], cs_v.shape[0]
    last = 4 * fine_slots
    flag_ref[...] = jnp.zeros(flag_ref.shape, F32)

    def fine(j, _):
        index = (fs_v, ft_v, fo_v, firsts[0])
        count_slot(j, fine_column, *index, n_v, h_v, table, 4 * j, out_sems.at[j], flag_ref, 0, ftt, fst, 128)
        return 0

    def coarse(j, _):
        index = (cs_v, ct_v, co_v, firsts[1])
        sem = out_sems.at[fine_slots + j]
        count_slot(j, coarse_column, *index, n_v, h_v, table, last + j, sem, flag_ref, fine_slots, ctt, cst, 64)
        return 0

    lax.fori_loop(0, fine_slots, fine, 0)
    lax.fori_loop(0, coarse_slots, coarse, 0)
    flag_v[...] = flag_ref[...].astype(BF)
    pltpu.sync_copy(flag_v, table.at[n_v.shape[0], 0:16, :])
    for j in range(fine_slots):
        at = pl.ds(4 * j, 4)
        pltpu.make_async_copy(n_v.at[at], table.at[at], out_sems.at[j]).wait()
    for j in range(coarse_slots):
        at = pl.ds(last + j, 1)
        pltpu.make_async_copy(n_v.at[at], table.at[at], out_sems.at[fine_slots + j]).wait()


def counts(firsts, fine_index, coarse_index, fine_boxes, coarse_boxes):
    fine_slots, fine_pairs = fine_index[0].shape
    coarse_slots, coarse_pairs = coarse_index[0].shape
    planes = 4 * fine_slots + coarse_slots
    sds = jax.ShapeDtypeStruct
    arrays = (*fine_index, *coarse_index)
    return pl.pallas_call(
        count_kernel,
        out_shape=sds((2 * planes + 1, 1024, 128), BF),
        in_specs=[SMEM] + [HBM] * 6,
        out_specs=HBM,
        scratch_shapes=[pltpu.VMEM(a.shape, a.dtype) for a in arrays]
        + [
            pltpu.VMEM((fine_boxes, fine_pairs), BF),
            pltpu.VMEM((256, fine_pairs), BF),
            pltpu.VMEM((coarse_boxes, coarse_pairs), BF),
            pltpu.VMEM((128, coarse_pairs), BF),
            pltpu.VMEM((planes, 1024, 128), BF),
            pltpu.VMEM((4, 1024, 128), BF),
            pltpu.VMEM((16, 128), F32),
            pltpu.VMEM((16, 128), BF),
            pltpu.SemaphoreType.DMA((6,)),
            pltpu.SemaphoreType.DMA((fine_slots + coarse_slots,)),
        ],
        cost_estimate=pl.CostEstimate(flops=9_000_000_000, bytes_accessed=8_000_000, transcendentals=0),
        name="counts",
    )(firsts, *arrays)


def apply_level(window, slots, n_ref, table, plane, flag_ref, flag_at, op_ref, out_ref, parts, boxes):
    split_ref, total_ref, waits, flag_wait, sem = parts
    count = slots * boxes
    wide = boxes // 64
    lane = lax.broadcasted_iota(jnp.int32, (128 * wide, 256), 1)
    many = 512 // boxes
    planes = 8 // many * wide
    depth = NOP // 2 * C

    def sources(slot):
        block = window(slot)
        turned = pltpu.roll(block, 64 if slot % 2 == 0 else 192, 1)
        left, right = (block, turned) if slot % 2 == 0 else (turned, block)
        return jnp.where(lane < C, left, 0.0).astype(BF), jnp.where(lane >= 64, right, 0.0).astype(BF)

    def weights(odd):
        start = [odd * 128 + k * 2 * C for k in range(NOP // 2)]
        return jnp.concatenate([op_ref[:, a : a + 256] for a in start], axis=0)

    def split(slot, sides, g):
        at = plane + slot * planes + g * wide
        pick = lambda rows: jnp.concatenate([n_ref[at + k, rows, :] for k in range(wide)], axis=1)
        first = jnp.dot(pick(slice(0, 512)), sides[0], preferred_element_type=F32)
        second = jnp.dot(pick(slice(512, 1024)), sides[1], preferred_element_type=F32)
        value = jnp.concatenate([first[:, :128], first[:, 128:] + second[:, :128], second[:, 128:]], axis=1)
        high = value.astype(BF)
        low = (value - high.astype(F32)).astype(BF)
        for k in range(many):
            lanes = slice((g * many + k) * 2 * C, (g * many + k + 1) * 2 * C)
            rows = slice(k * boxes, (k + 1) * boxes)
            split_ref[slot * boxes : (slot + 1) * boxes, lanes] = high[rows]
            split_ref[count + slot * boxes : count + (slot + 1) * boxes, lanes] = low[rows]

    for slot in range(slots):
        sides = sources(slot)
        for g in range(8 // many):
            waits[plane + slot * planes + g * wide].wait()
            split(slot, sides, g)
    for odd in range(2):
        total = jnp.dot(split_ref[:, odd * depth : (odd + 1) * depth], weights(odd), preferred_element_type=F32)
        total_ref[odd] = total[:count] + total[count:]
    if flag_at == 0:
        flag_wait.wait()

    @pl.when(jnp.max(flag_ref[...].astype(F32)) > 0.0)
    def _():
        for slot in range(slots):
            for first in (slot * boxes, count + slot * boxes):
                split_ref[first : first + boxes, :] = jnp.zeros((boxes, 2 * depth), BF)

            @pl.when(jnp.max(flag_ref[...].astype(F32)[flag_at + slot : flag_at + slot + 1, :]) > 0.0)
            def _(slot=slot):
                at = plane + slot * planes
                copy = pltpu.make_async_copy(
                    table.at[pl.ds(at + n_ref.shape[0] + 1, planes)], n_ref.at[pl.ds(at, planes)], sem
                )
                copy.start()
                copy.wait()
                sides = sources(slot)
                for g in range(8 // many):
                    split(slot, sides, g)

        for odd in range(2):
            extra = jnp.dot(split_ref[:, odd * depth : (odd + 1) * depth], weights(odd), preferred_element_type=F32)
            total_ref[odd] = total_ref[odd] + 256.0 * (extra[:count] + extra[count:])

    low_lanes = lax.broadcasted_iota(jnp.int32, (boxes, 128), 1) < 64
    for pair in range(slots // 2):
        rows = [slice((2 * pair + k) * boxes, (2 * pair + k + 1) * boxes) for k in range(2)]
        left = total_ref[0, rows[0], :] + pltpu.roll(total_ref[1, rows[0], :], 192, 1)
        right = total_ref[1, rows[1], :] + pltpu.roll(total_ref[0, rows[1], :], 64, 1)
        middle = jnp.where(low_lanes, left[:, 128:], right[:, :128])
        for k, piece in enumerate((left[:, :128], middle, right[:, 128:])):
            at = pair * 2 * C + k * 128
            out_ref[:, at : at + 128] = piece.astype(BF)


def apply_kernel(
    recv, table, fop, cop, fine_out, coarse_out, n_v, flag_ref, fine_v, coarse_v, split_ref, total, sems
):
    fine_slots, coarse_slots = fine_out.shape[1] // C, coarse_out.shape[1] // C
    last = 4 * fine_slots
    waits = {}
    for p in [*range(0, last, 2), *range(last, last + coarse_slots)]:
        at = slice(p, p + (2 if p < last else 1))
        waits[p] = pltpu.make_async_copy(table.at[at], n_v.at[at], sems.at[p])
        waits[p].start()
    flag_wait = pltpu.make_async_copy(table.at[n_v.shape[0], 0:16, :], flag_ref, sems.at[1])
    flag_wait.start()
    parts = (split_ref, total, waits, flag_wait, sems.at[5])

    def fine_window(slot):
        at = (slot % 2) * 128
        return recv[:, 0:16, at : at + 256].reshape(256, 256).astype(F32)

    def coarse_window(slot):
        at = (slot % 2) * 128
        own = recv[:, 16:24, at : at + 256].astype(F32)
        halo = recv[:, 24:32, at : at + 256].astype(F32)
        top = lax.broadcasted_iota(jnp.int32, own.shape, 1) < 4
        if slot < 2:
            both = jnp.where(top, own, pltpu.roll(halo, 4, 1))
        else:
            both = jnp.where(top, pltpu.roll(own, 4, 1), halo)
        return both.reshape(128, 256)

    apply_level(fine_window, fine_slots, n_v, table, 0, flag_ref, 0, fop, fine_v, parts, 128)
    done = pltpu.make_async_copy(fine_v, fine_out, sems.at[3])
    done.start()
    apply_level(coarse_window, coarse_slots, n_v, table, last, flag_ref, fine_slots, cop, coarse_v, parts, 64)
    pltpu.sync_copy(coarse_v, coarse_out)
    done.wait()


def apply(recv, table, fine_operators, coarse_operators, fine_shape, coarse_shape):
    rows = fine_shape[0] * fine_shape[1] // C
    outs = (jax.ShapeDtypeStruct(fine_shape, BF), jax.ShapeDtypeStruct(coarse_shape, BF))
    planes = table.shape[0] // 2
    return pl.pallas_call(
        apply_kernel,
        out_shape=outs,
        in_specs=[VMEM, HBM, VMEM, VMEM],
        out_specs=(HBM, HBM),
        scratch_shapes=[
            pltpu.VMEM((planes, 1024, 128), BF),
            pltpu.VMEM((16, 128), BF),
            pltpu.VMEM(fine_shape, BF),
            pltpu.VMEM(coarse_shape, BF),
            pltpu.VMEM((2 * rows, NOP * C), BF),
            pltpu.VMEM((2, rows, 256), F32),
            pltpu.SemaphoreType.DMA((planes,)),
        ],
        compiler_params=pltpu.CompilerParams(vmem_limit_bytes=LIMIT),
        cost_estimate=pl.CostEstimate(flops=3_000_000_000, bytes_accessed=8_000_000, transcendentals=0),
        name="apply",
    )(recv, table, fine_operators, coarse_operators)


def per_device(
    fine_density,
    coarse_density,
    fine_operators,
    coarse_operators,
    fine_balance,
    coarse_balance,
    fine_sources,
    fine_targets,
    fine_op_ids,
    coarse_sources,
    coarse_targets,
    coarse_op_ids,
):
    peers = lax.axis_size("dir")
    count = lax.axis_size("box")
    half = peers // 2
    fine_boxes = fine_density.shape[0] * peers
    coarse_boxes = coarse_density.shape[0] * peers
    position = lax.axis_index("box")
    firsts = jnp.stack([position * fine_boxes, position * coarse_boxes]).astype(jnp.int32)
    route = [(b * peers + d, (b + 1) * peers + d) for b in range(count - 1) for d in range(half, peers)]
    route += [(b * peers + d, (b - 1) * peers + d) for b in range(1, count) for d in range(half)]
    coarse_near = lax.ppermute(coarse_density, ("box", "dir"), route)
    fine_near = lax.ppermute(fine_density, ("box", "dir"), route)
    packed = pack(fine_balance, coarse_balance, fine_density, coarse_density, fine_near, coarse_near, peers)
    firsts, packed = lax.optimization_barrier((firsts, packed))
    recv = lax.all_to_all(packed, "dir", split_axis=0, concat_axis=0, tiled=True)
    table = counts(
        firsts,
        (fine_sources, fine_targets, fine_op_ids),
        (coarse_sources, coarse_targets, coarse_op_ids),
        fine_boxes,
        coarse_boxes,
    )
    fine_shape = (fine_boxes, fine_sources.shape[0] * C)
    coarse_shape = (coarse_boxes, coarse_sources.shape[0] * C)
    return apply(recv, table, fine_operators, coarse_operators, fine_shape, coarse_shape)


def solution(mesh):
    placed = (
        P(("box", "dir"), None),
        P(("box", "dir"), None),
        P(),
        P(),
        P(),
        P(),
        P("dir", "box"),
        P("dir", "box"),
        P("dir", "box"),
        P("dir", "box"),
        P("dir", "box"),
        P("dir", "box"),
    )
    return jax.shard_map(
        per_device,
        mesh=mesh,
        in_specs=placed,
        out_specs=(P("box", "dir"), P("box", "dir")),
        check_vma=False,
    )
```

```python
import functools

import jax
import jax.numpy as jnp
from jax import lax
from jax.experimental import pallas as pl
from jax.experimental.pallas import tpu as pltpu
from jax.sharding import PartitionSpec as P

RIM = 32
C = 192
NOP = 16
BF = jnp.bfloat16
F32 = jnp.float32


LIMIT = 50 << 20
MERGE_LIMIT = 56200000
BASE = 4096.0
VMEM = pl.BlockSpec(memory_space=pltpu.VMEM)
SMEM = pl.BlockSpec(memory_space=pltpu.SMEM)
HBM = pl.BlockSpec(memory_space=pltpu.HBM)


def fetch(pairs, sems, first=0):
    copies = [pltpu.make_async_copy(s, d, sems.at[first + i]) for i, (s, d) in enumerate(pairs)]
    for copy in copies:
        copy.start()
    return copies


def pack_kernel(fb, cb, fd, cd, sorted_ref, packed_ref, fb_s, cb_s, fd_v, cd_v, out_v, fine_wide, coarse_wide, sems):
    copies = fetch(((fb, fb_s), (cb, cb_s), (fd, fd_v), (cd, cd_v)), sems)
    for copy in copies:
        copy.wait()
    fine_wide[...] = fd_v[...].astype(F32)
    rows = cd_v[...].astype(F32)
    coarse_wide[0:4, :] = rows
    coarse_wide[4:8, :] = rows
    low = lax.broadcasted_iota(jnp.int32, (8, 128), 1) < 64
    top = lax.broadcasted_iota(jnp.int32, (8, 128), 0) < 4

    def window(ref, wedge):
        odd = lax.rem(wedge, 2)
        start = pl.multiple_of(wedge * C - odd * 64, 128)
        first = ref[:, pl.ds(start, 128)]
        second = ref[:, pl.ds(pl.multiple_of(start + 128, 128), 128)]
        return odd == 1, first, second, pltpu.roll(first, 64, 1), pltpu.roll(second, 64, 1)

    def left(ref, wedge):
        odd, first, second, first_r, second_r = window(ref, wedge)
        head = jnp.where(odd, jnp.where(low, first_r, second_r), first)
        return head, jnp.where(odd, second_r, second)

    def right(ref, wedge):
        odd, first, second, first_r, second_r = window(ref, wedge)
        tail = jnp.where(odd, second, jnp.where(low, first_r, second_r))
        return jnp.where(odd, first, first_r), tail

    def joined(even, odd):
        return even[0], jnp.where(low, even[1], odd[0]), odd[1]

    for peer in range(out_v.shape[0]):
        parts = joined(left(fine_wide, fb_s[2 * peer]), right(fine_wide, fb_s[2 * peer + 1]))
        upper = joined(left(coarse_wide, cb_s[4 * peer]), right(coarse_wide, cb_s[4 * peer + 1]))
        lower = joined(left(coarse_wide, cb_s[4 * peer + 2]), right(coarse_wide, cb_s[4 * peer + 3]))
        for k in range(3):
            lanes = slice(k * 128, (k + 1) * 128)
            out_v[peer, 0:8, lanes] = parts[k].astype(BF)
            out_v[peer, 8:16, lanes] = jnp.where(top, upper[k], lower[k]).astype(BF)
    copies = fetch(
        (
            (out_v, sorted_ref),
            (out_v.at[:, 0:8, :], packed_ref.at[:, 0:8, :]),
            (out_v.at[:, 8:16, :], packed_ref.at[:, 16:24, :]),
        ),
        sems,
    )
    for copy in copies:
        copy.wait()


def pack(fine_balance, coarse_balance, fine, coarse, peers):
    sds = jax.ShapeDtypeStruct
    return pl.pallas_call(
        pack_kernel,
        out_shape=(sds((peers, 16, 2 * C), BF), sds((peers, 32, 2 * C), BF)),
        in_specs=[HBM] * 4,
        out_specs=(HBM, HBM),
        scratch_shapes=[
            pltpu.SMEM(fine_balance.shape, jnp.int32),
            pltpu.SMEM(coarse_balance.shape, jnp.int32),
            pltpu.VMEM(fine.shape, BF),
            pltpu.VMEM(coarse.shape, BF),
            pltpu.VMEM((peers, 16, 2 * C), BF),
            pltpu.VMEM((8, fine.shape[1]), F32),
            pltpu.VMEM((8, coarse.shape[1]), F32),
            pltpu.SemaphoreType.DMA((4,)),
        ],
        cost_estimate=pl.CostEstimate(flops=4_000_000, bytes_accessed=800_000, transcendentals=0),
        name="pack",
    )(fine_balance, coarse_balance, fine, coarse)


def merge_kernel(near, _, packed_ref, sems):
    copies = fetch(
        (
            (near.at[:, 0:8, :], packed_ref.at[:, 8:16, :]),
            (near.at[:, 8:16, :], packed_ref.at[:, 24:32, :]),
        ),
        sems,
    )
    for copy in copies:
        copy.wait()


def merge(near, packed):
    return pl.pallas_call(
        merge_kernel,
        out_shape=jax.ShapeDtypeStruct(packed.shape, BF),
        in_specs=[VMEM, HBM],
        out_specs=HBM,
        scratch_shapes=[pltpu.SemaphoreType.DMA((2,))],
        input_output_aliases={1: 0},
        compiler_params=pltpu.CompilerParams(vmem_limit_bytes=MERGE_LIMIT),
        cost_estimate=pl.CostEstimate(flops=0, bytes_accessed=400_000, transcendentals=0),
        name="merge",
    )(near, packed)


def count_slot(slot, column, src_ref, tgt_ref, op_ref, first, n_ref, h_ref, table, plane, sem, flag_ref, flag_at, tt, st, boxes):
    pairs = src_ref.shape[1]
    rows = lambda v: jnp.broadcast_to(v, (16, pairs))
    steps = lax.broadcasted_iota(jnp.int32, (16, 128), 0).astype(F32)
    one, zero = jnp.ones((), BF), jnp.zeros((), BF)

    def hot(value, block):
        want = jnp.concatenate([(steps + 16.0 * block).astype(BF)] * (pairs // 128), axis=1)
        return jnp.where(value == want, one, zero)

    target = rows(tgt_ref[pl.ds(slot, 1), :] - first).astype(F32).astype(BF)
    source = rows(column(src_ref[pl.ds(slot, 1), :] - first)).astype(F32).astype(BF)
    for k in range(boxes // 16):
        tt[k * 16 : (k + 1) * 16, :] = hot(target, k)
    for k in range(st.shape[0] // 16):
        st[k * 16 : (k + 1) * 16, :] = hot(source, k)
    ops = rows(op_ref[pl.ds(slot, 1), :])
    member = ((ops & 1) * 4 + (ops >> 2)).astype(F32).astype(BF)
    factor = jnp.where((ops & 2) > 0, BASE, 1.0).astype(BF)
    many = 512 // boxes
    wide = st.shape[0] // 128
    planes = 8 // many * wide

    def store(ref, first, g, side, value):
        for k in range(wide):
            ref[first + g * wide + k, side * 512 : (side + 1) * 512, :] = value[:, k * 128 : (k + 1) * 128].astype(BF)

    def count(g):
        parts = []
        for k in range(many):
            mask = jnp.where(member == jnp.asarray(g * many + k, BF), factor, zero)
            part = tt[...].reshape(boxes // 16, 16, pairs) * mask[None]
            parts.append(part.reshape(boxes, pairs))
        lhs = jnp.concatenate(parts, axis=0)
        both = lax.dot_general(lhs, st[...], (((1,), (1,)), ((), ())), preferred_element_type=F32)
        second = jnp.floor(both * (1.0 / BASE))
        return both - second * BASE, second

    most = jnp.float32(0.0)
    for g in range(8 // many):
        found = count(g)
        for side in range(2):
            store(n_ref, plane, g, side, found[side])
        most = jnp.maximum(most, jnp.max(jnp.maximum(found[0], found[1])))
    big = most > 256.0
    flag_ref[pl.ds(flag_at + slot, 1), :] = jnp.full((1, 128), big.astype(F32))

    @pl.when(big)
    def _():
        for g in range(8 // many):
            found = count(g)
            for side in range(2):
                high = jnp.floor(found[side] * (1.0 / 256.0))
                store(n_ref, plane, g, side, found[side] - high * 256.0)
                store(h_ref, 0, g, side, high)
        pltpu.sync_copy(h_ref.at[pl.ds(0, planes)], table.at[pl.ds(n_ref.shape[0] + 1 + plane, planes)])

    pltpu.make_async_copy(n_ref.at[pl.ds(plane, planes)], table.at[pl.ds(plane, planes)], sem).start()


def fine_column(at):
    halo = jnp.logical_or(at < 0, at >= 128).astype(jnp.int32)
    return ((at & 127) >> 3) * 16 + halo * 8 + (at & 7)


def coarse_column(at):
    halo = jnp.logical_or(at < 0, at >= 64).astype(jnp.int32)
    return ((at & 63) >> 2) * 8 + halo * 4 + (at & 3)


def count_kernel(
    firsts, fs, ft, fo, cs, ct, co, table,
    fs_v, ft_v, fo_v, cs_v, ct_v, co_v, ftt, fst, ctt, cst, n_v, h_v, flag_ref, flag_v, sems, out_sems,
):
    copies = fetch(((fs, fs_v), (ft, ft_v), (fo, fo_v), (cs, cs_v), (ct, ct_v), (co, co_v)), sems)
    for copy in copies:
        copy.wait()
    fine_slots, coarse_slots = fs_v.shape[0], cs_v.shape[0]
    last = 4 * fine_slots
    flag_ref[...] = jnp.zeros(flag_ref.shape, F32)

    def fine(j, _):
        index = (fs_v, ft_v, fo_v, firsts[0])
        count_slot(j, fine_column, *index, n_v, h_v, table, 4 * j, out_sems.at[j], flag_ref, 0, ftt, fst, 128)
        return 0

    def coarse(j, _):
        index = (cs_v, ct_v, co_v, firsts[1])
        sem = out_sems.at[fine_slots + j]
        count_slot(j, coarse_column, *index, n_v, h_v, table, last + j, sem, flag_ref, fine_slots, ctt, cst, 64)
        return 0

    lax.fori_loop(0, fine_slots, fine, 0)
    lax.fori_loop(0, coarse_slots, coarse, 0)
    flag_v[...] = flag_ref[...].astype(BF)
    pltpu.sync_copy(flag_v, table.at[n_v.shape[0], 0:16, :])
    for j in range(fine_slots):
        at = pl.ds(4 * j, 4)
        pltpu.make_async_copy(n_v.at[at], table.at[at], out_sems.at[j]).wait()
    for j in range(coarse_slots):
        at = pl.ds(last + j, 1)
        pltpu.make_async_copy(n_v.at[at], table.at[at], out_sems.at[fine_slots + j]).wait()


def counts(firsts, fine_index, coarse_index, fine_boxes, coarse_boxes):
    fine_slots, fine_pairs = fine_index[0].shape
    coarse_slots, coarse_pairs = coarse_index[0].shape
    planes = 4 * fine_slots + coarse_slots
    sds = jax.ShapeDtypeStruct
    arrays = (*fine_index, *coarse_index)
    return pl.pallas_call(
        count_kernel,
        out_shape=sds((2 * planes + 1, 1024, 128), BF),
        in_specs=[SMEM] + [HBM] * 6,
        out_specs=HBM,
        scratch_shapes=[pltpu.VMEM(a.shape, a.dtype) for a in arrays]
        + [
            pltpu.VMEM((fine_boxes, fine_pairs), BF),
            pltpu.VMEM((256, fine_pairs), BF),
            pltpu.VMEM((coarse_boxes, coarse_pairs), BF),
            pltpu.VMEM((128, coarse_pairs), BF),
            pltpu.VMEM((planes, 1024, 128), BF),
            pltpu.VMEM((4, 1024, 128), BF),
            pltpu.VMEM((16, 128), F32),
            pltpu.VMEM((16, 128), BF),
            pltpu.SemaphoreType.DMA((6,)),
            pltpu.SemaphoreType.DMA((fine_slots + coarse_slots,)),
        ],
        cost_estimate=pl.CostEstimate(flops=9_000_000_000, bytes_accessed=8_000_000, transcendentals=0),
        name="counts",
    )(firsts, *arrays)


def apply_level(window, slots, n_ref, table, plane, flag_ref, flag_at, op_ref, out_ref, parts, boxes):
    split_ref, total_ref, waits, flag_wait, sem = parts
    count = slots * boxes
    wide = boxes // 64
    lane = lax.broadcasted_iota(jnp.int32, (128 * wide, 256), 1)
    many = 512 // boxes
    planes = 8 // many * wide
    depth = NOP // 2 * C

    def sources(slot):
        block = window(slot)
        turned = pltpu.roll(block, 64 if slot % 2 == 0 else 192, 1)
        left, right = (block, turned) if slot % 2 == 0 else (turned, block)
        return jnp.where(lane < C, left, 0.0).astype(BF), jnp.where(lane >= 64, right, 0.0).astype(BF)

    def weights(odd):
        start = [odd * 128 + k * 2 * C for k in range(NOP // 2)]
        return jnp.concatenate([op_ref[:, a : a + 256] for a in start], axis=0)

    def split(slot, sides, g):
        at = plane + slot * planes + g * wide
        pick = lambda rows: jnp.concatenate([n_ref[at + k, rows, :] for k in range(wide)], axis=1)
        if wide == 1:
            both = jnp.concatenate([pick(slice(0, 512)), pick(slice(512, 1024))], axis=1)
            none = jnp.zeros((128, 128), BF)
            halves = [jnp.concatenate([sides[0], none], axis=1), jnp.concatenate([none, sides[1]], axis=1)]
            value = jnp.dot(both, jnp.concatenate(halves, axis=0), preferred_element_type=F32)
        else:
            first = jnp.dot(pick(slice(0, 512)), sides[0], preferred_element_type=F32)
            second = jnp.dot(pick(slice(512, 1024)), sides[1], preferred_element_type=F32)
            value = jnp.concatenate([first[:, :128], first[:, 128:] + second[:, :128], second[:, 128:]], axis=1)
        high = value.astype(BF)
        low = (value - high.astype(F32)).astype(BF)
        for k in range(many):
            lanes = slice((g * many + k) * 2 * C, (g * many + k + 1) * 2 * C)
            rows = slice(k * boxes, (k + 1) * boxes)
            split_ref[slot * boxes : (slot + 1) * boxes, lanes] = high[rows]
            split_ref[count + slot * boxes : count + (slot + 1) * boxes, lanes] = low[rows]

    for slot in range(slots):
        sides = sources(slot)
        for g in range(8 // many):
            waits[plane + slot * planes + g * wide].wait()
            split(slot, sides, g)
    for odd in range(2):
        total = jnp.dot(split_ref[:, odd * depth : (odd + 1) * depth], weights(odd), preferred_element_type=F32)
        total_ref[odd] = total[:count] + total[count:]
    if flag_at == 0:
        flag_wait.wait()

    @pl.when(jnp.max(flag_ref[...].astype(F32)) > 0.0)
    def _():
        for slot in range(slots):
            for first in (slot * boxes, count + slot * boxes):
                split_ref[first : first + boxes, :] = jnp.zeros((boxes, 2 * depth), BF)

            @pl.when(jnp.max(flag_ref[...].astype(F32)[flag_at + slot : flag_at + slot + 1, :]) > 0.0)
            def _(slot=slot):
                at = plane + slot * planes
                copy = pltpu.make_async_copy(
                    table.at[pl.ds(at + n_ref.shape[0] + 1, planes)], n_ref.at[pl.ds(at, planes)], sem
                )
                copy.start()
                copy.wait()
                sides = sources(slot)
                for g in range(8 // many):
                    split(slot, sides, g)

        for odd in range(2):
            extra = jnp.dot(split_ref[:, odd * depth : (odd + 1) * depth], weights(odd), preferred_element_type=F32)
            total_ref[odd] = total_ref[odd] + 256.0 * (extra[:count] + extra[count:])

    low_lanes = lax.broadcasted_iota(jnp.int32, (boxes, 128), 1) < 64
    for pair in range(slots // 2):
        rows = [slice((2 * pair + k) * boxes, (2 * pair + k + 1) * boxes) for k in range(2)]
        left = total_ref[0, rows[0], :] + pltpu.roll(total_ref[1, rows[0], :], 192, 1)
        right = total_ref[1, rows[1], :] + pltpu.roll(total_ref[0, rows[1], :], 64, 1)
        middle = jnp.where(low_lanes, left[:, 128:], right[:, :128])
        for k, piece in enumerate((left[:, :128], middle, right[:, 128:])):
            at = pair * 2 * C + k * 128
            out_ref[:, at : at + 128] = piece.astype(BF)


def apply_kernel(
    recv, table, fop, cop, fine_out, coarse_out, n_v, flag_ref, fine_v, coarse_v, split_ref, total, sems
):
    fine_slots, coarse_slots = fine_out.shape[1] // C, coarse_out.shape[1] // C
    last = 4 * fine_slots
    waits = {}
    for p in [*range(0, last, 2), *range(last, last + coarse_slots)]:
        at = slice(p, p + (2 if p < last else 1))
        waits[p] = pltpu.make_async_copy(table.at[at], n_v.at[at], sems.at[p])
        waits[p].start()
    flag_wait = pltpu.make_async_copy(table.at[n_v.shape[0], 0:16, :], flag_ref, sems.at[1])
    flag_wait.start()
    parts = (split_ref, total, waits, flag_wait, sems.at[5])

    def fine_window(slot):
        at = (slot % 2) * 128
        return recv[:, 0:16, at : at + 256].reshape(256, 256).astype(F32)

    def coarse_window(slot):
        at = (slot % 2) * 128
        own = recv[:, 16:24, at : at + 256].astype(F32)
        halo = recv[:, 24:32, at : at + 256].astype(F32)
        top = lax.broadcasted_iota(jnp.int32, own.shape, 1) < 4
        if slot < 2:
            both = jnp.where(top, own, pltpu.roll(halo, 4, 1))
        else:
            both = jnp.where(top, pltpu.roll(own, 4, 1), halo)
        return both.reshape(128, 256)

    apply_level(fine_window, fine_slots, n_v, table, 0, flag_ref, 0, fop, fine_v, parts, 128)
    done = pltpu.make_async_copy(fine_v, fine_out, sems.at[3])
    done.start()
    apply_level(coarse_window, coarse_slots, n_v, table, last, flag_ref, fine_slots, cop, coarse_v, parts, 64)
    pltpu.sync_copy(coarse_v, coarse_out)
    done.wait()


def apply(recv, table, fine_operators, coarse_operators, fine_shape, coarse_shape):
    rows = fine_shape[0] * fine_shape[1] // C
    outs = (jax.ShapeDtypeStruct(fine_shape, BF), jax.ShapeDtypeStruct(coarse_shape, BF))
    planes = table.shape[0] // 2
    return pl.pallas_call(
        apply_kernel,
        out_shape=outs,
        in_specs=[VMEM, HBM, VMEM, VMEM],
        out_specs=(HBM, HBM),
        scratch_shapes=[
            pltpu.VMEM((planes, 1024, 128), BF),
            pltpu.VMEM((16, 128), BF),
            pltpu.VMEM(fine_shape, BF),
            pltpu.VMEM(coarse_shape, BF),
            pltpu.VMEM((2 * rows, NOP * C), BF),
            pltpu.VMEM((2, rows, 256), F32),
            pltpu.SemaphoreType.DMA((planes,)),
        ],
        compiler_params=pltpu.CompilerParams(vmem_limit_bytes=LIMIT),
        cost_estimate=pl.CostEstimate(flops=3_000_000_000, bytes_accessed=8_000_000, transcendentals=0),
        name="apply",
    )(recv, table, fine_operators, coarse_operators)


def per_device(
    fine_density,
    coarse_density,
    fine_operators,
    coarse_operators,
    fine_balance,
    coarse_balance,
    fine_sources,
    fine_targets,
    fine_op_ids,
    coarse_sources,
    coarse_targets,
    coarse_op_ids,
):
    peers = lax.axis_size("dir")
    count = lax.axis_size("box")
    half = peers // 2
    fine_boxes = fine_density.shape[0] * peers
    coarse_boxes = coarse_density.shape[0] * peers
    position = lax.axis_index("box")
    firsts = jnp.stack([position * fine_boxes, position * coarse_boxes]).astype(jnp.int32)
    route = [(b * peers + d, (b + 1) * peers + d) for b in range(count - 1) for d in range(half, peers)]
    route += [(b * peers + d, (b - 1) * peers + d) for b in range(1, count) for d in range(half)]
    mine, packed = pack(fine_balance, coarse_balance, fine_density, coarse_density, peers)
    packed = merge(lax.ppermute(mine, ("box", "dir"), route), packed)
    firsts, packed = lax.optimization_barrier((firsts, packed))
    recv = lax.all_to_all(packed, "dir", split_axis=0, concat_axis=0, tiled=True)
    table = counts(
        firsts,
        (fine_sources, fine_targets, fine_op_ids),
        (coarse_sources, coarse_targets, coarse_op_ids),
        fine_boxes,
        coarse_boxes,
    )
    fine_shape = (fine_boxes, fine_sources.shape[0] * C)
    coarse_shape = (coarse_boxes, coarse_sources.shape[0] * C)
    return apply(recv, table, fine_operators, coarse_operators, fine_shape, coarse_shape)


def solution(mesh):
    placed = (
        P(("box", "dir"), None),
        P(("box", "dir"), None),
        P(),
        P(),
        P(),
        P(),
        P("dir", "box"),
        P("dir", "box"),
        P("dir", "box"),
        P("dir", "box"),
        P("dir", "box"),
        P("dir", "box"),
    )
    return jax.shard_map(
        per_device,
        mesh=mesh,
        in_specs=placed,
        out_specs=(P("box", "dir"), P("box", "dir")),
        check_vma=False,
    )
```

```python
import functools

import jax
import jax.numpy as jnp
from jax import lax
from jax.experimental import pallas as pl
from jax.experimental.pallas import tpu as pltpu
from jax.sharding import PartitionSpec as P

RIM = 32
C = 192
NOP = 16
BF = jnp.bfloat16
F32 = jnp.float32


LIMIT = 50 << 20
MERGE_LIMIT = 56200000
BASE = 4096.0
VMEM = pl.BlockSpec(memory_space=pltpu.VMEM)
SMEM = pl.BlockSpec(memory_space=pltpu.SMEM)
HBM = pl.BlockSpec(memory_space=pltpu.HBM)


def fetch(pairs, sems, first=0):
    copies = [pltpu.make_async_copy(s, d, sems.at[first + i]) for i, (s, d) in enumerate(pairs)]
    for copy in copies:
        copy.start()
    return copies


def pack_kernel(fb, cb, fd, cd, sorted_ref, packed_ref, fb_s, cb_s, fd_v, cd_v, out_v, fine_wide, coarse_wide, sems):
    copies = fetch(((fb, fb_s), (fd, fd_v), (cb, cb_s), (cd, cd_v)), sems)
    low = lax.broadcasted_iota(jnp.int32, (8, 128), 1) < 64
    top = lax.broadcasted_iota(jnp.int32, (8, 128), 0) < 4

    def window(ref, wedge):
        odd = lax.rem(wedge, 2)
        start = pl.multiple_of(wedge * C - odd * 64, 128)
        first = ref[:, pl.ds(start, 128)]
        second = ref[:, pl.ds(pl.multiple_of(start + 128, 128), 128)]
        return odd == 1, first, second, pltpu.roll(first, 64, 1), pltpu.roll(second, 64, 1)

    def left(ref, wedge):
        odd, first, second, first_r, second_r = window(ref, wedge)
        head = jnp.where(odd, jnp.where(low, first_r, second_r), first)
        return head, jnp.where(odd, second_r, second)

    def right(ref, wedge):
        odd, first, second, first_r, second_r = window(ref, wedge)
        tail = jnp.where(odd, second, jnp.where(low, first_r, second_r))
        return jnp.where(odd, first, first_r), tail

    def joined(even, odd):
        return even[0], jnp.where(low, even[1], odd[0]), odd[1]

    peers = out_v.shape[0]
    for copy in copies[:2]:
        copy.wait()
    fine_wide[...] = fd_v[...].astype(F32)
    for peer in range(peers):
        parts = joined(left(fine_wide, fb_s[2 * peer]), right(fine_wide, fb_s[2 * peer + 1]))
        for k in range(3):
            out_v[peer, 0:8, k * 128 : (k + 1) * 128] = parts[k].astype(BF)
    rows = slice(0, 8)
    fine_rows = out_v.at[:, rows, :]
    sent = fetch(((fine_rows, sorted_ref.at[:, rows, :]), (fine_rows, packed_ref.at[:, rows, :])), sems, 4)
    for copy in copies[2:]:
        copy.wait()
    coarse_half = cd_v[...].astype(F32)
    coarse_wide[0:4, :] = coarse_half
    coarse_wide[4:8, :] = coarse_half
    for group in range(0, peers, 4):
        for peer in range(group, group + 4):
            upper = joined(left(coarse_wide, cb_s[4 * peer]), right(coarse_wide, cb_s[4 * peer + 1]))
            lower = joined(left(coarse_wide, cb_s[4 * peer + 2]), right(coarse_wide, cb_s[4 * peer + 3]))
            for k in range(3):
                out_v[peer, 8:16, k * 128 : (k + 1) * 128] = jnp.where(top, upper[k], lower[k]).astype(BF)
        at = slice(group, group + 4)
        half = out_v.at[at, 8:16, :]
        pair = ((half, sorted_ref.at[at, 8:16, :]), (half, packed_ref.at[at, 16:24, :]))
        sent += fetch(pair, sems, 6 + group // 2)
    for copy in sent:
        copy.wait()


def pack(fine_balance, coarse_balance, fine, coarse, peers):
    sds = jax.ShapeDtypeStruct
    return pl.pallas_call(
        pack_kernel,
        out_shape=(sds((peers, 16, 2 * C), BF), sds((peers, 32, 2 * C), BF)),
        in_specs=[HBM] * 4,
        out_specs=(HBM, HBM),
        scratch_shapes=[
            pltpu.SMEM(fine_balance.shape, jnp.int32),
            pltpu.SMEM(coarse_balance.shape, jnp.int32),
            pltpu.VMEM(fine.shape, BF),
            pltpu.VMEM(coarse.shape, BF),
            pltpu.VMEM((peers, 16, 2 * C), BF),
            pltpu.VMEM((8, fine.shape[1]), F32),
            pltpu.VMEM((8, coarse.shape[1]), F32),
            pltpu.SemaphoreType.DMA((14,)),
        ],
        cost_estimate=pl.CostEstimate(flops=4_000_000, bytes_accessed=800_000, transcendentals=0),
        name="pack",
    )(fine_balance, coarse_balance, fine, coarse)


def merge_kernel(near, _, packed_ref, sems):
    copies = fetch(
        (
            (near.at[:, 0:8, :], packed_ref.at[:, 8:16, :]),
            (near.at[:, 8:16, :], packed_ref.at[:, 24:32, :]),
        ),
        sems,
    )
    for copy in copies:
        copy.wait()


def merge(near, packed):
    return pl.pallas_call(
        merge_kernel,
        out_shape=jax.ShapeDtypeStruct(packed.shape, BF),
        in_specs=[VMEM, HBM],
        out_specs=HBM,
        scratch_shapes=[pltpu.SemaphoreType.DMA((2,))],
        input_output_aliases={1: 0},
        compiler_params=pltpu.CompilerParams(vmem_limit_bytes=MERGE_LIMIT),
        cost_estimate=pl.CostEstimate(flops=0, bytes_accessed=400_000, transcendentals=0),
        name="merge",
    )(near, packed)


def count_slot(slot, column, src_ref, tgt_ref, op_ref, first, n_ref, h_ref, table, plane, sem, flag_ref, flag_at, tt, st, boxes):
    pairs = src_ref.shape[1]
    rows = lambda v: jnp.broadcast_to(v, (16, pairs))
    steps = lax.broadcasted_iota(jnp.int32, (16, 128), 0).astype(F32)
    one, zero = jnp.ones((), BF), jnp.zeros((), BF)

    def hot(value, block):
        want = jnp.concatenate([(steps + 16.0 * block).astype(BF)] * (pairs // 128), axis=1)
        return jnp.where(value == want, one, zero)

    target = rows(tgt_ref[pl.ds(slot, 1), :] - first).astype(F32).astype(BF)
    source = rows(column(src_ref[pl.ds(slot, 1), :] - first)).astype(F32).astype(BF)
    for k in range(boxes // 16):
        tt[k * 16 : (k + 1) * 16, :] = hot(target, k)
    for k in range(st.shape[0] // 16):
        st[k * 16 : (k + 1) * 16, :] = hot(source, k)
    ops = rows(op_ref[pl.ds(slot, 1), :])
    member = ((ops & 1) * 4 + (ops >> 2)).astype(F32).astype(BF)
    factor = jnp.where((ops & 2) > 0, BASE, 1.0).astype(BF)
    many = 512 // boxes
    wide = st.shape[0] // 128
    planes = 8 // many * wide

    def store(ref, first, g, side, value):
        for k in range(wide):
            ref[first + g * wide + k, side * 512 : (side + 1) * 512, :] = value[:, k * 128 : (k + 1) * 128].astype(BF)

    def count(g):
        parts = []
        for k in range(many):
            mask = jnp.where(member == jnp.asarray(g * many + k, BF), factor, zero)
            part = tt[...].reshape(boxes // 16, 16, pairs) * mask[None]
            parts.append(part.reshape(boxes, pairs))
        lhs = jnp.concatenate(parts, axis=0)
        both = lax.dot_general(lhs, st[...], (((1,), (1,)), ((), ())), preferred_element_type=F32)
        second = jnp.floor(both * (1.0 / BASE))
        return both - second * BASE, second

    most = jnp.float32(0.0)
    for g in range(8 // many):
        found = count(g)
        for side in range(2):
            store(n_ref, plane, g, side, found[side])
        most = jnp.maximum(most, jnp.max(jnp.maximum(found[0], found[1])))
    big = most > 256.0
    flag_ref[pl.ds(flag_at + slot, 1), :] = jnp.full((1, 128), big.astype(F32))

    @pl.when(big)
    def _():
        for g in range(8 // many):
            found = count(g)
            for side in range(2):
                high = jnp.floor(found[side] * (1.0 / 256.0))
                store(n_ref, plane, g, side, found[side] - high * 256.0)
                store(h_ref, 0, g, side, high)
        pltpu.sync_copy(h_ref.at[pl.ds(0, planes)], table.at[pl.ds(n_ref.shape[0] + 1 + plane, planes)])

    pltpu.make_async_copy(n_ref.at[pl.ds(plane, planes)], table.at[pl.ds(plane, planes)], sem).start()


def fine_column(at):
    halo = jnp.logical_or(at < 0, at >= 128).astype(jnp.int32)
    return ((at & 127) >> 3) * 16 + halo * 8 + (at & 7)


def coarse_column(at):
    halo = jnp.logical_or(at < 0, at >= 64).astype(jnp.int32)
    return ((at & 63) >> 2) * 8 + halo * 4 + (at & 3)


def count_kernel(
    firsts, fs, ft, fo, cs, ct, co, table,
    fs_v, ft_v, fo_v, cs_v, ct_v, co_v, ftt, fst, ctt, cst, n_v, h_v, flag_ref, flag_v, sems, out_sems,
):
    copies = fetch(((fs, fs_v), (ft, ft_v), (fo, fo_v), (cs, cs_v), (ct, ct_v), (co, co_v)), sems)
    for copy in copies:
        copy.wait()
    fine_slots, coarse_slots = fs_v.shape[0], cs_v.shape[0]
    last = 4 * fine_slots
    flag_ref[...] = jnp.zeros(flag_ref.shape, F32)

    def fine(j, _):
        index = (fs_v, ft_v, fo_v, firsts[0])
        count_slot(j, fine_column, *index, n_v, h_v, table, 4 * j, out_sems.at[j], flag_ref, 0, ftt, fst, 128)
        return 0

    def coarse(j, _):
        index = (cs_v, ct_v, co_v, firsts[1])
        sem = out_sems.at[fine_slots + j]
        count_slot(j, coarse_column, *index, n_v, h_v, table, last + j, sem, flag_ref, fine_slots, ctt, cst, 64)
        return 0

    lax.fori_loop(0, fine_slots, fine, 0)
    lax.fori_loop(0, coarse_slots, coarse, 0)
    flag_v[...] = flag_ref[...].astype(BF)
    pltpu.sync_copy(flag_v, table.at[n_v.shape[0], 0:16, :])
    for j in range(fine_slots):
        at = pl.ds(4 * j, 4)
        pltpu.make_async_copy(n_v.at[at], table.at[at], out_sems.at[j]).wait()
    for j in range(coarse_slots):
        at = pl.ds(last + j, 1)
        pltpu.make_async_copy(n_v.at[at], table.at[at], out_sems.at[fine_slots + j]).wait()


def counts(firsts, fine_index, coarse_index, fine_boxes, coarse_boxes):
    fine_slots, fine_pairs = fine_index[0].shape
    coarse_slots, coarse_pairs = coarse_index[0].shape
    planes = 4 * fine_slots + coarse_slots
    sds = jax.ShapeDtypeStruct
    arrays = (*fine_index, *coarse_index)
    return pl.pallas_call(
        count_kernel,
        out_shape=sds((2 * planes + 1, 1024, 128), BF),
        in_specs=[SMEM] + [HBM] * 6,
        out_specs=HBM,
        scratch_shapes=[pltpu.VMEM(a.shape, a.dtype) for a in arrays]
        + [
            pltpu.VMEM((fine_boxes, fine_pairs), BF),
            pltpu.VMEM((256, fine_pairs), BF),
            pltpu.VMEM((coarse_boxes, coarse_pairs), BF),
            pltpu.VMEM((128, coarse_pairs), BF),
            pltpu.VMEM((planes, 1024, 128), BF),
            pltpu.VMEM((4, 1024, 128), BF),
            pltpu.VMEM((16, 128), F32),
            pltpu.VMEM((16, 128), BF),
            pltpu.SemaphoreType.DMA((6,)),
            pltpu.SemaphoreType.DMA((fine_slots + coarse_slots,)),
        ],
        cost_estimate=pl.CostEstimate(flops=9_000_000_000, bytes_accessed=8_000_000, transcendentals=0),
        name="counts",
    )(firsts, *arrays)


class Level:
    def __init__(self, window, n_ref, plane, flag_ref, flag_at, table, op_ref, out_ref, split_ref, total_ref, boxes):
        self.window, self.n_ref, self.plane, self.table = window, n_ref, plane, table
        self.flag_ref, self.flag_at = flag_ref, flag_at
        self.op_ref, self.out_ref, self.split_ref, self.total_ref = op_ref, out_ref, split_ref, total_ref
        self.boxes = boxes
        self.count = split_ref.shape[0] // 2
        self.slots = self.count // boxes
        self.wide = boxes // 64
        self.many = 512 // boxes
        self.planes = 8 // self.many * self.wide
        self.depth = NOP // 2 * C

    def sources(self, slot):
        lane = lax.broadcasted_iota(jnp.int32, (128 * self.wide, 256), 1)
        block = self.window(slot)
        turned = pltpu.roll(block, 64 if slot % 2 == 0 else 192, 1)
        left, right = (block, turned) if slot % 2 == 0 else (turned, block)
        return jnp.where(lane < C, left, 0.0).astype(BF), jnp.where(lane >= 64, right, 0.0).astype(BF)

    def weights(self, odd):
        start = [odd * 128 + k * 2 * C for k in range(NOP // 2)]
        return jnp.concatenate([self.op_ref[:, a : a + 256] for a in start], axis=0)

    def split(self, slot, sides, ref, plane, g):
        at = plane + g * self.wide
        pick = lambda rows: jnp.concatenate([ref[at + k, rows, :] for k in range(self.wide)], axis=1)
        if self.wide == 1:
            both = jnp.concatenate([pick(slice(0, 512)), pick(slice(512, 1024))], axis=1)
            none = jnp.zeros((128, 128), BF)
            halves = [jnp.concatenate([sides[0], none], axis=1), jnp.concatenate([none, sides[1]], axis=1)]
            value = jnp.dot(both, jnp.concatenate(halves, axis=0), preferred_element_type=F32)
        else:
            first = jnp.dot(pick(slice(0, 512)), sides[0], preferred_element_type=F32)
            second = jnp.dot(pick(slice(512, 1024)), sides[1], preferred_element_type=F32)
            value = jnp.concatenate([first[:, :128], first[:, 128:] + second[:, :128], second[:, 128:]], axis=1)
        high = value.astype(BF)
        low = (value - high.astype(F32)).astype(BF)
        many, boxes = self.many, self.boxes
        for k in range(many):
            lanes = slice((g * many + k) * 2 * C, (g * many + k + 1) * 2 * C)
            rows = slice(k * boxes, (k + 1) * boxes)
            self.split_ref[slot * boxes : (slot + 1) * boxes, lanes] = high[rows]
            self.split_ref[self.count + slot * boxes : self.count + (slot + 1) * boxes, lanes] = low[rows]

    def gather(self, waits):
        for slot in range(self.slots):
            sides = self.sources(slot)
            for g in range(8 // self.many):
                if waits:
                    waits[slot * 8 // self.many + g].wait()
                self.split(slot, sides, self.n_ref, self.plane + slot * self.planes, g)

    def operate(self, odd):
        at = slice(odd * self.depth, (odd + 1) * self.depth)
        total = jnp.dot(self.split_ref[:, at], self.weights(odd), preferred_element_type=F32)
        return total[: self.count] + total[self.count :]

    def translate(self):
        for odd in range(2):
            self.total_ref[odd] = self.operate(odd)

    def add_high(self, h_v, sem):
        boxes, planes = self.boxes, self.planes

        flags = slice(self.flag_at, self.flag_at + self.slots)

        @pl.when(jnp.max(self.flag_ref[...].astype(F32)[flags]) > 0.0)
        def _():
            for slot in range(self.slots):
                for first in (slot * boxes, self.count + slot * boxes):
                    self.split_ref[first : first + boxes, :] = jnp.zeros((boxes, 2 * self.depth), BF)

                at = self.flag_at + slot

                @pl.when(jnp.max(self.flag_ref[...].astype(F32)[at : at + 1, :]) > 0.0)
                def _(slot=slot):
                    first = self.n_ref.shape[0] + 1 + self.plane + slot * planes
                    copy = pltpu.make_async_copy(self.table.at[pl.ds(first, planes)], h_v.at[pl.ds(0, planes)], sem)
                    copy.start()
                    copy.wait()
                    sides = self.sources(slot)
                    for g in range(8 // self.many):
                        self.split(slot, sides, h_v, 0, g)

            for odd in range(2):
                self.total_ref[odd] = self.total_ref[odd] + 256.0 * self.operate(odd)

    def finish(self):
        boxes = self.boxes
        low_lanes = lax.broadcasted_iota(jnp.int32, (boxes, 128), 1) < 64
        for pair in range(self.slots // 2):
            rows = [slice((2 * pair + k) * boxes, (2 * pair + k + 1) * boxes) for k in range(2)]
            left = self.total_ref[0, rows[0], :] + pltpu.roll(self.total_ref[1, rows[0], :], 192, 1)
            right = self.total_ref[1, rows[1], :] + pltpu.roll(self.total_ref[0, rows[1], :], 64, 1)
            middle = jnp.where(low_lanes, left[:, 128:], right[:, :128])
            for k, piece in enumerate((left[:, :128], middle, right[:, 128:])):
                at = pair * 2 * C + k * 128
                self.out_ref[:, at : at + 128] = piece.astype(BF)


def apply_kernel(
    recv, table, fop, cop, fine_out, coarse_out,
    n_v, flag_v, fine_o, coarse_o, fine_split, coarse_split, fine_total, coarse_total, h_v, sems,
):
    fine_slots, coarse_slots = fine_out.shape[1] // C, coarse_out.shape[1] // C
    last = 4 * fine_slots
    pieces = [slice(p, p + 2) for p in range(0, last, 2)]
    fine_waits = fetch([(table.at[p], n_v.at[p]) for p in pieces], sems, 2)
    tail = slice(last, last + coarse_slots)
    rest = [(table.at[n_v.shape[0], 0:16, :], flag_v), (table.at[tail], n_v.at[tail])]
    rest = fetch(rest, sems, 2 + len(pieces))

    def fine_window(slot):
        at = (slot % 2) * 128
        return recv[:, 0:16, at : at + 256].reshape(256, 256).astype(F32)

    def coarse_window(slot):
        at = (slot % 2) * 128
        own = recv[:, 16:24, at : at + 256].astype(F32)
        halo = recv[:, 24:32, at : at + 256].astype(F32)
        top = lax.broadcasted_iota(jnp.int32, own.shape, 1) < 4
        if slot < 2:
            both = jnp.where(top, own, pltpu.roll(halo, 4, 1))
        else:
            both = jnp.where(top, pltpu.roll(own, 4, 1), halo)
        return both.reshape(128, 256)

    ends = ((fine_o, fine_split, fine_total, 128), (coarse_o, coarse_split, coarse_total, 64))
    fine = Level(fine_window, n_v, 0, flag_v, 0, table, fop, *ends[0])
    coarse = Level(coarse_window, n_v, last, flag_v, fine_slots, table, cop, *ends[1])
    fine.gather(fine_waits)
    for copy in rest:
        copy.wait()
    fine.translate()
    coarse.gather([])
    coarse.translate()
    fine.add_high(h_v, sems.at[0])
    coarse.add_high(h_v, sems.at[0])
    fine.finish()
    done = pltpu.make_async_copy(fine_o, fine_out, sems.at[1])
    done.start()
    coarse.finish()
    pltpu.sync_copy(coarse_o, coarse_out)
    done.wait()


def apply(recv, table, fine_operators, coarse_operators, fine_shape, coarse_shape):
    rows = fine_shape[0] * fine_shape[1] // C
    outs = (jax.ShapeDtypeStruct(fine_shape, BF), jax.ShapeDtypeStruct(coarse_shape, BF))
    planes = table.shape[0] // 2
    return pl.pallas_call(
        apply_kernel,
        out_shape=outs,
        in_specs=[VMEM, HBM, VMEM, VMEM],
        out_specs=(HBM, HBM),
        scratch_shapes=[
            pltpu.VMEM((planes, 1024, 128), BF),
            pltpu.VMEM((16, 128), BF),
            pltpu.VMEM(fine_shape, BF),
            pltpu.VMEM(coarse_shape, BF),
            pltpu.VMEM((2 * rows, NOP * C), BF),
            pltpu.VMEM((2 * rows, NOP * C), BF),
            pltpu.VMEM((2, rows, 256), F32),
            pltpu.VMEM((2, rows, 256), F32),
            pltpu.VMEM((4, 1024, 128), BF),
            pltpu.SemaphoreType.DMA((8,)),
        ],
        compiler_params=pltpu.CompilerParams(vmem_limit_bytes=LIMIT),
        cost_estimate=pl.CostEstimate(flops=3_000_000_000, bytes_accessed=8_000_000, transcendentals=0),
        name="apply",
    )(recv, table, fine_operators, coarse_operators)


def per_device(
    fine_density,
    coarse_density,
    fine_operators,
    coarse_operators,
    fine_balance,
    coarse_balance,
    fine_sources,
    fine_targets,
    fine_op_ids,
    coarse_sources,
    coarse_targets,
    coarse_op_ids,
):
    peers = lax.axis_size("dir")
    count = lax.axis_size("box")
    half = peers // 2
    fine_boxes = fine_density.shape[0] * peers
    coarse_boxes = coarse_density.shape[0] * peers
    position = lax.axis_index("box")
    firsts = jnp.stack([position * fine_boxes, position * coarse_boxes]).astype(jnp.int32)
    route = [(b * peers + d, (b + 1) * peers + d) for b in range(count - 1) for d in range(half, peers)]
    route += [(b * peers + d, (b - 1) * peers + d) for b in range(1, count) for d in range(half)]
    mine, packed = pack(fine_balance, coarse_balance, fine_density, coarse_density, peers)
    packed = merge(lax.ppermute(mine, ("box", "dir"), route), packed)
    firsts, packed = lax.optimization_barrier((firsts, packed))
    recv = lax.all_to_all(packed, "dir", split_axis=0, concat_axis=0, tiled=True)
    table = counts(
        firsts,
        (fine_sources, fine_targets, fine_op_ids),
        (coarse_sources, coarse_targets, coarse_op_ids),
        fine_boxes,
        coarse_boxes,
    )
    fine_shape = (fine_boxes, fine_sources.shape[0] * C)
    coarse_shape = (coarse_boxes, coarse_sources.shape[0] * C)
    return apply(recv, table, fine_operators, coarse_operators, fine_shape, coarse_shape)


def solution(mesh):
    placed = (
        P(("box", "dir"), None),
        P(("box", "dir"), None),
        P(),
        P(),
        P(),
        P(),
        P("dir", "box"),
        P("dir", "box"),
        P("dir", "box"),
        P("dir", "box"),
        P("dir", "box"),
        P("dir", "box"),
    )
    return jax.shard_map(
        per_device,
        mesh=mesh,
        in_specs=placed,
        out_specs=(P("box", "dir"), P("box", "dir")),
        check_vma=False,
    )
```

```python
import functools

import jax
import jax.numpy as jnp
from jax import lax
from jax.experimental import pallas as pl
from jax.experimental.pallas import tpu as pltpu
from jax.sharding import PartitionSpec as P

RIM = 32
C = 192
NOP = 16
BF = jnp.bfloat16
F32 = jnp.float32


LIMIT = 50 << 20
MERGE_LIMIT = 56200000
BASE = 4096.0
VMEM = pl.BlockSpec(memory_space=pltpu.VMEM)
SMEM = pl.BlockSpec(memory_space=pltpu.SMEM)
HBM = pl.BlockSpec(memory_space=pltpu.HBM)


def fetch(pairs, sems, first=0):
    copies = [pltpu.make_async_copy(s, d, sems.at[first + i]) for i, (s, d) in enumerate(pairs)]
    for copy in copies:
        copy.start()
    return copies


def pack_kernel(fb, cb, fd, cd, sorted_ref, packed_ref, fb_s, cb_s, fd_v, cd_v, out_v, fine_wide, coarse_wide, sems):
    copies = fetch(((fb, fb_s), (fd, fd_v), (cb, cb_s), (cd, cd_v)), sems)
    low = lax.broadcasted_iota(jnp.int32, (8, 128), 1) < 64
    top = lax.broadcasted_iota(jnp.int32, (8, 128), 0) < 4

    def window(ref, wedge):
        odd = lax.rem(wedge, 2)
        start = pl.multiple_of(wedge * C - odd * 64, 128)
        first = ref[:, pl.ds(start, 128)]
        second = ref[:, pl.ds(pl.multiple_of(start + 128, 128), 128)]
        return odd == 1, first, second, pltpu.roll(first, 64, 1), pltpu.roll(second, 64, 1)

    def left(ref, wedge):
        odd, first, second, first_r, second_r = window(ref, wedge)
        head = jnp.where(odd, jnp.where(low, first_r, second_r), first)
        return head, jnp.where(odd, second_r, second)

    def right(ref, wedge):
        odd, first, second, first_r, second_r = window(ref, wedge)
        tail = jnp.where(odd, second, jnp.where(low, first_r, second_r))
        return jnp.where(odd, first, first_r), tail

    def joined(even, odd):
        return even[0], jnp.where(low, even[1], odd[0]), odd[1]

    peers = out_v.shape[0]
    for copy in copies[:2]:
        copy.wait()
    fine_wide[...] = fd_v[...].astype(F32)
    for peer in range(peers):
        parts = joined(left(fine_wide, fb_s[2 * peer]), right(fine_wide, fb_s[2 * peer + 1]))
        for k in range(3):
            out_v[peer, 0:8, k * 128 : (k + 1) * 128] = parts[k].astype(BF)
    rows = slice(0, 8)
    fine_rows = out_v.at[:, rows, :]
    sent = fetch(((fine_rows, sorted_ref.at[:, rows, :]), (fine_rows, packed_ref.at[:, rows, :])), sems, 4)
    for copy in copies[2:]:
        copy.wait()
    coarse_half = cd_v[...].astype(F32)
    coarse_wide[0:4, :] = coarse_half
    coarse_wide[4:8, :] = coarse_half
    for group in range(0, peers, 4):
        for peer in range(group, group + 4):
            upper = joined(left(coarse_wide, cb_s[4 * peer]), right(coarse_wide, cb_s[4 * peer + 1]))
            lower = joined(left(coarse_wide, cb_s[4 * peer + 2]), right(coarse_wide, cb_s[4 * peer + 3]))
            for k in range(3):
                out_v[peer, 8:16, k * 128 : (k + 1) * 128] = jnp.where(top, upper[k], lower[k]).astype(BF)
        at = slice(group, group + 4)
        half = out_v.at[at, 8:16, :]
        pair = ((half, sorted_ref.at[at, 8:16, :]), (half, packed_ref.at[at, 16:24, :]))
        sent += fetch(pair, sems, 6 + group // 2)
    for copy in sent:
        copy.wait()


def pack(fine_balance, coarse_balance, fine, coarse, peers):
    sds = jax.ShapeDtypeStruct
    return pl.pallas_call(
        pack_kernel,
        out_shape=(sds((peers, 16, 2 * C), BF), sds((peers, 32, 2 * C), BF)),
        in_specs=[HBM] * 4,
        out_specs=(HBM, HBM),
        scratch_shapes=[
            pltpu.SMEM(fine_balance.shape, jnp.int32),
            pltpu.SMEM(coarse_balance.shape, jnp.int32),
            pltpu.VMEM(fine.shape, BF),
            pltpu.VMEM(coarse.shape, BF),
            pltpu.VMEM((peers, 16, 2 * C), BF),
            pltpu.VMEM((8, fine.shape[1]), F32),
            pltpu.VMEM((8, coarse.shape[1]), F32),
            pltpu.SemaphoreType.DMA((14,)),
        ],
        cost_estimate=pl.CostEstimate(flops=4_000_000, bytes_accessed=800_000, transcendentals=0),
        name="pack",
    )(fine_balance, coarse_balance, fine, coarse)


def merge_kernel(near, _, packed_ref, sems):
    copies = fetch(
        (
            (near.at[:, 0:8, :], packed_ref.at[:, 8:16, :]),
            (near.at[:, 8:16, :], packed_ref.at[:, 24:32, :]),
        ),
        sems,
    )
    for copy in copies:
        copy.wait()


def merge(near, packed):
    return pl.pallas_call(
        merge_kernel,
        out_shape=jax.ShapeDtypeStruct(packed.shape, BF),
        in_specs=[VMEM, HBM],
        out_specs=HBM,
        scratch_shapes=[pltpu.SemaphoreType.DMA((2,))],
        input_output_aliases={1: 0},
        compiler_params=pltpu.CompilerParams(vmem_limit_bytes=MERGE_LIMIT),
        cost_estimate=pl.CostEstimate(flops=0, bytes_accessed=400_000, transcendentals=0),
        name="merge",
    )(near, packed)


def count_slot(slot, column, src_ref, tgt_ref, op_ref, first, n_ref, h_ref, table, plane, sem, flag_ref, flag_at, tt, st, boxes):
    pairs = src_ref.shape[1]
    rows = lambda v: jnp.broadcast_to(v, (16, pairs))
    steps = lax.broadcasted_iota(jnp.int32, (16, 128), 0).astype(F32)
    one, zero = jnp.ones((), BF), jnp.zeros((), BF)

    def hot(value, block):
        want = jnp.concatenate([(steps + 16.0 * block).astype(BF)] * (pairs // 128), axis=1)
        return jnp.where(value == want, one, zero)

    target = rows(tgt_ref[pl.ds(slot, 1), :] - first).astype(F32).astype(BF)
    source = rows(column(src_ref[pl.ds(slot, 1), :] - first)).astype(F32).astype(BF)
    for k in range(boxes // 16):
        tt[k * 16 : (k + 1) * 16, :] = hot(target, k)
    for k in range(st.shape[0] // 16):
        st[k * 16 : (k + 1) * 16, :] = hot(source, k)
    ops = rows(op_ref[pl.ds(slot, 1), :])
    member = ((ops & 1) * 4 + (ops >> 2)).astype(F32).astype(BF)
    factor = jnp.where((ops & 2) > 0, BASE, 1.0).astype(BF)
    many = 512 // boxes
    wide = st.shape[0] // 128
    planes = 8 // many * wide

    def store(ref, first, g, side, value):
        for k in range(wide):
            ref[first + g * wide + k, side * 512 : (side + 1) * 512, :] = value[:, k * 128 : (k + 1) * 128].astype(BF)

    def count(g):
        parts = []
        for k in range(many):
            mask = jnp.where(member == jnp.asarray(g * many + k, BF), factor, zero)
            part = tt[...].reshape(boxes // 16, 16, pairs) * mask[None]
            parts.append(part.reshape(boxes, pairs))
        lhs = jnp.concatenate(parts, axis=0)
        both = lax.dot_general(lhs, st[...], (((1,), (1,)), ((), ())), preferred_element_type=F32)
        second = jnp.floor(both * (1.0 / BASE))
        return both - second * BASE, second

    most = jnp.float32(0.0)
    for g in range(8 // many):
        found = count(g)
        for side in range(2):
            store(n_ref, plane, g, side, found[side])
        most = jnp.maximum(most, jnp.max(jnp.maximum(found[0], found[1])))
    big = most > 256.0
    flag_ref[pl.ds(flag_at + slot, 1), :] = jnp.full((1, 128), big.astype(F32))

    @pl.when(big)
    def _():
        for g in range(8 // many):
            found = count(g)
            for side in range(2):
                high = jnp.floor(found[side] * (1.0 / 256.0))
                store(n_ref, plane, g, side, found[side] - high * 256.0)
                store(h_ref, 0, g, side, high)
        pltpu.sync_copy(h_ref.at[pl.ds(0, planes)], table.at[pl.ds(n_ref.shape[0] + 1 + plane, planes)])

    pltpu.make_async_copy(n_ref.at[pl.ds(plane, planes)], table.at[pl.ds(plane, planes)], sem).start()


def fine_column(at):
    halo = jnp.logical_or(at < 0, at >= 128).astype(jnp.int32)
    return ((at & 127) >> 3) * 16 + halo * 8 + (at & 7)


def coarse_column(at):
    halo = jnp.logical_or(at < 0, at >= 64).astype(jnp.int32)
    return ((at & 63) >> 2) * 8 + halo * 4 + (at & 3)


def count_kernel(
    firsts, fs, ft, fo, cs, ct, co, table,
    fs_v, ft_v, fo_v, cs_v, ct_v, co_v, ftt, fst, ctt, cst, n_v, h_v, flag_ref, flag_v, sems, out_sems,
):
    copies = fetch(((fs, fs_v), (ft, ft_v), (fo, fo_v), (cs, cs_v), (ct, ct_v), (co, co_v)), sems)
    for copy in copies:
        copy.wait()
    fine_slots, coarse_slots = fs_v.shape[0], cs_v.shape[0]
    last = 4 * fine_slots
    flag_ref[...] = jnp.zeros(flag_ref.shape, F32)

    def fine(j, _):
        index = (fs_v, ft_v, fo_v, firsts[0])
        count_slot(j, fine_column, *index, n_v, h_v, table, 4 * j, out_sems.at[j], flag_ref, 0, ftt, fst, 128)
        return 0

    def coarse(j, _):
        index = (cs_v, ct_v, co_v, firsts[1])
        sem = out_sems.at[fine_slots + j]
        count_slot(j, coarse_column, *index, n_v, h_v, table, last + j, sem, flag_ref, fine_slots, ctt, cst, 64)
        return 0

    lax.fori_loop(0, fine_slots, fine, 0)
    lax.fori_loop(0, coarse_slots, coarse, 0)
    flag_v[...] = flag_ref[...].astype(BF)
    pltpu.sync_copy(flag_v, table.at[n_v.shape[0], 0:16, :])
    for j in range(fine_slots):
        at = pl.ds(4 * j, 4)
        pltpu.make_async_copy(n_v.at[at], table.at[at], out_sems.at[j]).wait()
    for j in range(coarse_slots):
        at = pl.ds(last + j, 1)
        pltpu.make_async_copy(n_v.at[at], table.at[at], out_sems.at[fine_slots + j]).wait()


def counts(firsts, fine_index, coarse_index, fine_boxes, coarse_boxes):
    fine_slots, fine_pairs = fine_index[0].shape
    coarse_slots, coarse_pairs = coarse_index[0].shape
    planes = 4 * fine_slots + coarse_slots
    sds = jax.ShapeDtypeStruct
    arrays = (*fine_index, *coarse_index)
    return pl.pallas_call(
        count_kernel,
        out_shape=sds((2 * planes + 1, 1024, 128), BF),
        in_specs=[SMEM] + [HBM] * 6,
        out_specs=HBM,
        scratch_shapes=[pltpu.VMEM(a.shape, a.dtype) for a in arrays]
        + [
            pltpu.VMEM((fine_boxes, fine_pairs), BF),
            pltpu.VMEM((256, fine_pairs), BF),
            pltpu.VMEM((coarse_boxes, coarse_pairs), BF),
            pltpu.VMEM((128, coarse_pairs), BF),
            pltpu.VMEM((planes, 1024, 128), BF),
            pltpu.VMEM((4, 1024, 128), BF),
            pltpu.VMEM((16, 128), F32),
            pltpu.VMEM((16, 128), BF),
            pltpu.SemaphoreType.DMA((6,)),
            pltpu.SemaphoreType.DMA((fine_slots + coarse_slots,)),
        ],
        cost_estimate=pl.CostEstimate(flops=9_000_000_000, bytes_accessed=8_000_000, transcendentals=0),
        name="counts",
    )(firsts, *arrays)


class Level:
    def __init__(self, window, n_ref, plane, flag_ref, flag_at, table, op_ref, out_ref, split_ref, total_ref, boxes):
        self.window, self.n_ref, self.plane, self.table = window, n_ref, plane, table
        self.flag_ref, self.flag_at = flag_ref, flag_at
        self.op_ref, self.out_ref, self.split_ref, self.total_ref = op_ref, out_ref, split_ref, total_ref
        self.boxes = boxes
        self.count = split_ref.shape[0] // 2
        self.slots = self.count // boxes
        self.wide = boxes // 64
        self.many = 512 // boxes
        self.planes = 8 // self.many * self.wide
        self.depth = NOP // 2 * C

    def sources(self, slot):
        lane = lax.broadcasted_iota(jnp.int32, (128 * self.wide, 256), 1)
        block = self.window(slot)
        turned = pltpu.roll(block, 64 if slot % 2 == 0 else 192, 1)
        left, right = (block, turned) if slot % 2 == 0 else (turned, block)
        return jnp.where(lane < C, left, 0.0).astype(BF), jnp.where(lane >= 64, right, 0.0).astype(BF)

    def weights(self, odd):
        start = [odd * 128 + k * 2 * C for k in range(NOP // 2)]
        return jnp.concatenate([self.op_ref[:, a : a + 256] for a in start], axis=0)

    def split(self, slot, sides, ref, plane, g):
        at = plane + g * self.wide
        pick = lambda rows: jnp.concatenate([ref[at + k, rows, :] for k in range(self.wide)], axis=1)
        if self.wide == 1:
            both = jnp.concatenate([pick(slice(0, 512)), pick(slice(512, 1024))], axis=1)
            none = jnp.zeros((128, 128), BF)
            halves = [jnp.concatenate([sides[0], none], axis=1), jnp.concatenate([none, sides[1]], axis=1)]
            value = jnp.dot(both, jnp.concatenate(halves, axis=0), preferred_element_type=F32)
        else:
            first = jnp.dot(pick(slice(0, 512)), sides[0], preferred_element_type=F32)
            second = jnp.dot(pick(slice(512, 1024)), sides[1], preferred_element_type=F32)
            value = jnp.concatenate([first[:, :128], first[:, 128:] + second[:, :128], second[:, 128:]], axis=1)
        high = value.astype(BF)
        low = (value - high.astype(F32)).astype(BF)
        many, boxes = self.many, self.boxes
        for k in range(many):
            lanes = slice((g * many + k) * 2 * C, (g * many + k + 1) * 2 * C)
            rows = slice(k * boxes, (k + 1) * boxes)
            self.split_ref[slot * boxes : (slot + 1) * boxes, lanes] = high[rows]
            self.split_ref[self.count + slot * boxes : self.count + (slot + 1) * boxes, lanes] = low[rows]

    def gather(self, waits):
        for slot in range(self.slots):
            sides = self.sources(slot)
            for g in range(8 // self.many):
                if waits:
                    waits[slot * 8 // self.many + g].wait()
                self.split(slot, sides, self.n_ref, self.plane + slot * self.planes, g)

    def operate(self, odd):
        at = slice(odd * self.depth, (odd + 1) * self.depth)
        total = jnp.dot(self.split_ref[:, at], self.weights(odd), preferred_element_type=F32)
        return total[: self.count] + total[self.count :]

    def translate(self):
        for odd in range(2):
            self.total_ref[odd] = self.operate(odd)

    def add_high(self, h_v, sem):
        boxes, planes = self.boxes, self.planes

        for slot in range(self.slots):
            for first in (slot * boxes, self.count + slot * boxes):
                self.split_ref[first : first + boxes, :] = jnp.zeros((boxes, 2 * self.depth), BF)
            at = self.flag_at + slot

            @pl.when(jnp.max(self.flag_ref[...].astype(F32)[at : at + 1, :]) > 0.0)
            def _(slot=slot):
                first = self.n_ref.shape[0] + 1 + self.plane + slot * planes
                copy = pltpu.make_async_copy(self.table.at[pl.ds(first, planes)], h_v.at[pl.ds(0, planes)], sem)
                copy.start()
                copy.wait()
                sides = self.sources(slot)
                for g in range(8 // self.many):
                    self.split(slot, sides, h_v, 0, g)

        for odd in range(2):
            self.total_ref[odd] = self.total_ref[odd] + 256.0 * self.operate(odd)

    def finish(self):
        boxes = self.boxes
        low_lanes = lax.broadcasted_iota(jnp.int32, (boxes, 128), 1) < 64
        for pair in range(self.slots // 2):
            rows = [slice((2 * pair + k) * boxes, (2 * pair + k + 1) * boxes) for k in range(2)]
            left = self.total_ref[0, rows[0], :] + pltpu.roll(self.total_ref[1, rows[0], :], 192, 1)
            right = self.total_ref[1, rows[1], :] + pltpu.roll(self.total_ref[0, rows[1], :], 64, 1)
            middle = jnp.where(low_lanes, left[:, 128:], right[:, :128])
            for k, piece in enumerate((left[:, :128], middle, right[:, 128:])):
                at = pair * 2 * C + k * 128
                self.out_ref[:, at : at + 128] = piece.astype(BF)


def apply_kernel(
    recv, table, fop, cop, fine_out, coarse_out,
    n_v, flag_v, fine_o, coarse_o, fine_split, coarse_split, fine_total, coarse_total, h_v, sems,
):
    fine_slots, coarse_slots = fine_out.shape[1] // C, coarse_out.shape[1] // C
    last = 4 * fine_slots
    flag_copy = fetch([(table.at[n_v.shape[0], 0:16, :], flag_v)], sems)[0]
    pieces = [slice(p, p + 2) for p in range(0, last, 2)]
    ahead = len(pieces)
    pieces += [slice(last, last + coarse_slots)]
    waits = fetch([(table.at[p], n_v.at[p]) for p in pieces], sems, 2)

    def fine_window(slot):
        at = (slot % 2) * 128
        return recv[:, 0:16, at : at + 256].reshape(256, 256).astype(F32)

    def coarse_window(slot):
        at = (slot % 2) * 128
        own = recv[:, 16:24, at : at + 256].astype(F32)
        halo = recv[:, 24:32, at : at + 256].astype(F32)
        top = lax.broadcasted_iota(jnp.int32, own.shape, 1) < 4
        if slot < 2:
            both = jnp.where(top, own, pltpu.roll(halo, 4, 1))
        else:
            both = jnp.where(top, pltpu.roll(own, 4, 1), halo)
        return both.reshape(128, 256)

    ends = ((fine_o, fine_split, fine_total, 128), (coarse_o, coarse_split, coarse_total, 64))
    fine = Level(fine_window, n_v, 0, flag_v, 0, table, fop, *ends[0])
    coarse = Level(coarse_window, n_v, last, flag_v, fine_slots, table, cop, *ends[1])
    flag_copy.wait()
    some = jnp.max(flag_v[...].astype(F32)) > 0.0
    fine.gather(waits[:ahead])
    waits[ahead].wait()
    fine.translate()
    coarse.gather([])
    coarse.translate()

    @pl.when(some)
    def _():
        coarse.add_high(h_v, sems.at[0])
        fine.add_high(h_v, sems.at[0])

    fine.finish()
    done = fetch([(fine_o, fine_out)], sems)
    coarse.finish()
    done += fetch([(coarse_o, coarse_out)], sems, 1)
    for copy in done:
        copy.wait()


def apply(recv, table, fine_operators, coarse_operators, fine_shape, coarse_shape):
    rows = fine_shape[0] * fine_shape[1] // C
    outs = (jax.ShapeDtypeStruct(fine_shape, BF), jax.ShapeDtypeStruct(coarse_shape, BF))
    planes = table.shape[0] // 2
    return pl.pallas_call(
        apply_kernel,
        out_shape=outs,
        in_specs=[VMEM, HBM, VMEM, VMEM],
        out_specs=(HBM, HBM),
        scratch_shapes=[
            pltpu.VMEM((planes, 1024, 128), BF),
            pltpu.VMEM((16, 128), BF),
            pltpu.VMEM(fine_shape, BF),
            pltpu.VMEM(coarse_shape, BF),
            pltpu.VMEM((2 * rows, NOP * C), BF),
            pltpu.VMEM((2 * rows, NOP * C), BF),
            pltpu.VMEM((2, rows, 256), F32),
            pltpu.VMEM((2, rows, 256), F32),
            pltpu.VMEM((4, 1024, 128), BF),
            pltpu.SemaphoreType.DMA((12,)),
        ],
        compiler_params=pltpu.CompilerParams(vmem_limit_bytes=LIMIT),
        cost_estimate=pl.CostEstimate(flops=3_000_000_000, bytes_accessed=8_000_000, transcendentals=0),
        name="apply",
    )(recv, table, fine_operators, coarse_operators)


def per_device(
    fine_density,
    coarse_density,
    fine_operators,
    coarse_operators,
    fine_balance,
    coarse_balance,
    fine_sources,
    fine_targets,
    fine_op_ids,
    coarse_sources,
    coarse_targets,
    coarse_op_ids,
):
    peers = lax.axis_size("dir")
    count = lax.axis_size("box")
    half = peers // 2
    fine_boxes = fine_density.shape[0] * peers
    coarse_boxes = coarse_density.shape[0] * peers
    position = lax.axis_index("box")
    firsts = jnp.stack([position * fine_boxes, position * coarse_boxes]).astype(jnp.int32)
    route = [(b * peers + d, (b + 1) * peers + d) for b in range(count - 1) for d in range(half, peers)]
    route += [(b * peers + d, (b - 1) * peers + d) for b in range(1, count) for d in range(half)]
    mine, packed = pack(fine_balance, coarse_balance, fine_density, coarse_density, peers)
    packed = merge(lax.ppermute(mine, ("box", "dir"), route), packed)
    firsts, packed = lax.optimization_barrier((firsts, packed))
    recv = lax.all_to_all(packed, "dir", split_axis=0, concat_axis=0, tiled=True)
    table = counts(
        firsts,
        (fine_sources, fine_targets, fine_op_ids),
        (coarse_sources, coarse_targets, coarse_op_ids),
        fine_boxes,
        coarse_boxes,
    )
    fine_shape = (fine_boxes, fine_sources.shape[0] * C)
    coarse_shape = (coarse_boxes, coarse_sources.shape[0] * C)
    return apply(recv, table, fine_operators, coarse_operators, fine_shape, coarse_shape)


def solution(mesh):
    placed = (
        P(("box", "dir"), None),
        P(("box", "dir"), None),
        P(),
        P(),
        P(),
        P(),
        P("dir", "box"),
        P("dir", "box"),
        P("dir", "box"),
        P("dir", "box"),
        P("dir", "box"),
        P("dir", "box"),
    )
    return jax.shard_map(
        per_device,
        mesh=mesh,
        in_specs=placed,
        out_specs=(P("box", "dir"), P("box", "dir")),
        check_vma=False,
    )
```
